256 devices in a mesh: sec: 2 (over y_lo), grp: 16 (over z, y_hi), tp: 8 (over x, core).
Axes of the slice: x: 4, y: 4 (y_hi: 2, y_lo: 2; y = y_hi * 2 + y_lo), z: 8, core: 2. Of those that a mesh axis runs over, the one named last changes fastest.
Arguments:
- hidden_in: bfloat16 [1024, 7168], P(('sec', 'grp', 'tp')), may hold values from -6 to 6
- queries: bfloat16 [1024, 16, 8, 576], P(('sec', 'grp'), None, 'tp'), may hold values from -61 to 61
- latent_cache: bfloat16 [1024, 64, 576], P(('sec', 'grp')), may hold values from -6 to 6
- lengths: int32 [1024], P(('sec', 'grp')), may hold values from 2 to 64, as said below
- w_uv: bfloat16 [16, 8, 512, 128], P(None, 'tp'), may hold values from -0.75 to 0.75
- attn_weight: bfloat16 [16, 8, 128, 7168], P(None, 'tp', None, 'grp'), may hold values from -0.125 to 0.125
- norm_gain: float32 [7168], replicated, may hold values from 0.1 to 1.9
- router: bfloat16 [7168, 32], replicated, may hold values from -0.0625 to 0.0625
- routes: int32 [1024, 8], P(('sec', 'grp', 'tp')), may hold values from 0 to 31, all different within a row; in each aligned block of 4 rows (0 to 3, 4 to 7, ...) at most 2 rows name the same one
- live_counts: int32 [256], P(('sec', 'grp', 'tp')), may hold values from 3 to 4, as said below
- expert_in: bfloat16 [32, 7168, 2, 1024], P(('sec', 'grp'), None, None, 'tp'), may hold values from -0.0625 to 0.0625
- expert_out: bfloat16 [32, 1024, 7168], P(('sec', 'grp'), 'tp'), may hold values from -0.5 to 0.5
Outputs:
- layer_out: bfloat16 [1024, 7168], P(('sec', 'grp', 'tp'))
The draws below stay inside these ranges and needn't reach their ends.
Inputs may be any that keep to these rules, and one draw needn't show every extreme that they name: `lengths`: some request has exactly 64 cached positions and some has 2. `live_counts`: some device has all 4 slots live and some has exactly 3. `routes`: the 8 experts of a token differ. Within the rows of one device (aligned blocks of 4 rows) no expert is named by more than 2 rows, a bound that some block reaches.
All inputs are finite; a program needn't handle non-finite values.
Results may differ from the reference program's by a relative error of at most 0.018.
Values may be sent and summed in bfloat16 or wider, within the bound.
No kernel may reach another device: no remote copies, remote signals or barrier semaphores. Data moves between devices by JAX's collectives and lax.ppermute only.
A program may use at most 64 MiB of HBM per device.

```python
import math
import jax
import jax.numpy as jnp
import numpy as np
from jax import lax

D = 7168
HEADS = 128
KV_RANK = 512
V_DIM = 128
HID = 1024
TOKENS_PER_UNIT = 4
CACHE_LEN = 64
QK_DIM = 576
HEAD_BLOCK = 16
TOKENS = 1024
EXPERTS = 32
TOPK = 8
MOST = 2
N_TP = 8


def draw_queries(key, part):
    shape = (TOKENS, HEAD_BLOCK, HEADS // HEAD_BLOCK, QK_DIM)
    query_key = jax.random.fold_in(key, 1)
    values = jnp.clip(jax.random.normal(query_key, shape, jnp.float32), -6.0, 6.0)
    return values.astype(jnp.bfloat16)


def draw_latent_cache(key, part):
    shape = (TOKENS, CACHE_LEN, QK_DIM)
    cache_key = jax.random.fold_in(key, 2)
    values = jnp.clip(jax.random.normal(cache_key, shape, jnp.float32), -6.0, 6.0)
    return values.astype(jnp.bfloat16)


def draw_lengths(key, part):
    drawn = jax.random.randint(jax.random.fold_in(key, 11), (TOKENS,), 2, CACHE_LEN + 1)
    longest = jax.random.randint(jax.random.fold_in(key, 12), (), 0, TOKENS)
    shortest = (longest + 1 + jax.random.randint(jax.random.fold_in(key, 13), (), 0, TOKENS - 1)) % TOKENS
    return drawn.at[shortest].set(2).at[longest].set(CACHE_LEN).astype(jnp.int32)


def draw_live_counts(key, part):
    devices_total = TOKENS // TOKENS_PER_UNIT
    smallest_value = 3 * TOKENS_PER_UNIT // 4
    drawn = jax.random.randint(jax.random.fold_in(key, 21), (devices_total,), smallest_value, TOKENS_PER_UNIT + 1)
    fullest = jax.random.randint(jax.random.fold_in(key, 22), (), 0, devices_total)
    emptiest = (fullest + 1 + jax.random.randint(jax.random.fold_in(key, 23), (), 0, devices_total - 1)) % devices_total
    return drawn.at[emptiest].set(smallest_value).at[fullest].set(TOKENS_PER_UNIT).astype(jnp.int32)


def level_of(rng, extent, cuts, smallest, largest):
    level, own = 1.0, jax.random.fold_in(rng, 6)
    for dim, blocks in cuts:
        heights = jnp.exp(jax.random.uniform(jax.random.fold_in(own, dim), (blocks,), jnp.float32, smallest / len(cuts), largest / len(cuts)))
        level = level * jnp.repeat(heights, extent[dim] // blocks).reshape([-1 if axis == dim else 1 for axis in range(len(extent))])
    return level


def assign_block(stream_key, own, number, rows, amount, top, limit, slope):
    sequence = jax.random.permutation(stream_key, amount)
    heavy_load, ordinary = load_shares(amount, rows * top, limit, slope, True), load_shares(amount, rows * top, limit, slope, False)
    places = jnp.arange(amount)

    def named(sizes, offset_by):
        used = int((sizes > 0).sum())
        fixed = max(1, used // 4)
        shifted = fixed + (places - fixed + offset_by * (used - fixed)) % max(1, amount - fixed)
        return jnp.zeros((amount,), jnp.int32).at[sequence[jnp.where(places < fixed, places, shifted)]].set(jnp.asarray(sizes, jnp.int32))

    sizes = jnp.where(number % 4 == 0, named(heavy_load, number // 4), named(ordinary, number - number // 4 - 1))
    mixed = jax.random.permutation(jax.random.fold_in(own, 3), amount)
    giver, sink = mixed[0:amount // 2 * 2:2], mixed[1:amount // 2 * 2:2]
    slack = jnp.minimum(sizes[giver] - 1, limit - sizes[sink]) // 2
    slack = jnp.where((giver == sequence[0]) | (sink == sequence[0]) | (sizes[sink] == 0), 0, jnp.maximum(slack, 0))
    shifted = jax.random.randint(jax.random.fold_in(own, 4), (amount // 2,), 0, 1 << 20) % (slack + 1)
    sizes = sizes.at[giver].add(-shifted).at[sink].add(shifted)
    items = jnp.searchsorted(jnp.cumsum(sizes), jnp.arange(rows * top), side="right").astype(jnp.int32)
    table = items.reshape(top, rows).T
    table = table[jax.random.permutation(jax.random.fold_in(own, 1), rows)]
    offset_by = jax.random.randint(jax.random.fold_in(own, 2), (rows, 1), 0, top)
    return jnp.take_along_axis(table, (jnp.arange(top)[None, :] + offset_by) % top, axis=1)


def load_shares(amount, total, most, skew, full):
    portions = [(1 << 20) // math.isqrt(grade ** skew) + 1 for grade in range(1, amount + 1)]
    largest = most if full else min(most, max(-(-total // amount), total * portions[0] // sum(portions)))
    least = 1 if total - largest >= amount - 1 else 0
    holding, surplus = [largest] + [least] * (amount - 1), total - largest - least * (amount - 1)
    while surplus > 0:
        candidates = [i for i in range(1, amount) if holding[i] < largest] or [i for i in range(1, amount) if holding[i] < most]
        whole, left = sum([portions[i] for i in candidates]), surplus
        for i in candidates:
            more = min(most - holding[i], max(1, left * portions[i] // whole), surplus)
            holding[i] = holding[i] + more
            surplus = surplus - more
    return np.array(holding)


def gaussian(key, dims, width, bound, shards=(), kind=jnp.bfloat16):
    values = jax.random.normal(key, dims, jnp.float32) * width
    if len(shards) > 0:
        values = level_of(key, dims, shards, -0.22, 0.18) * values
    return jnp.clip(values, min=-bound, max=bound).astype(kind)


def setup_inputs(seed: int = 0) -> dict:
    key_list = jax.random.split(jax.random.key(seed), 13)
    hidden_in = gaussian(key_list[0], (TOKENS, D), 1.0, 6.0, ((0, 256),))
    queries = draw_queries(jax.random.fold_in(key_list[12], 71), 0)
    latent_cache = draw_latent_cache(jax.random.fold_in(key_list[12], 71), 0)
    lengths = draw_lengths(jax.random.fold_in(key_list[12], 71), 0)
    w_uv = gaussian(key_list[4], (HEAD_BLOCK, HEADS // HEAD_BLOCK, KV_RANK, V_DIM), (KV_RANK // 8) ** -0.5, 0.75, ((1, 8),))
    attn_weight = gaussian(key_list[5], (HEAD_BLOCK, HEADS // HEAD_BLOCK, V_DIM, D), (HEAD_BLOCK * V_DIM) ** -0.5, 0.125, ((1, 8), (3, 16)))
    norm_gain = jnp.clip(1.0 + 0.18 * jax.random.normal(key_list[6], (D,), jnp.float32), 0.1, 1.9)
    router = gaussian(key_list[7], (D, EXPERTS), D ** -0.5, 0.0625)
    routes_keys = jax.random.split(jax.random.fold_in(key_list[8], 1), TOKENS // TOKENS_PER_UNIT)
    routes_turns = jax.random.permutation(jax.random.fold_in(key_list[8], 3), TOKENS // TOKENS_PER_UNIT)
    routes = jax.vmap(lambda own, number: assign_block(jax.random.fold_in(key_list[8], 2), own, number, TOKENS_PER_UNIT, EXPERTS, TOPK, MOST, 2))(routes_keys, routes_turns).reshape((TOKENS, TOPK))
    live_counts = draw_live_counts(jax.random.fold_in(key_list[12], 71), 0)
    expert_in = gaussian(key_list[10], (EXPERTS, D, 2, HID), D ** -0.5, 0.0625, ((0, 32), (3, 8)))
    expert_out = gaussian(key_list[11], (EXPERTS, HID, D), (HID // 8) ** -0.5, 0.5, ((0, 32), (1, 8)))
    return dict(hidden_in=hidden_in, queries=queries, latent_cache=latent_cache, lengths=lengths, w_uv=w_uv, attn_weight=attn_weight, norm_gain=norm_gain, router=router, routes=routes, live_counts=live_counts, expert_in=expert_in, expert_out=expert_out)


score_scale = 192.0 ** (-0.5)
route_scale = 2.5

def routed_experts(normalized_input, routes, gate_weights, expert_in, expert_out):
    pair_total = TOKENS * TOPK
    pair_expert = routes.reshape(pair_total).astype(jnp.int32)
    pair_token = (jnp.arange(pair_total) // TOPK).astype(jnp.int32)
    pair_gate = gate_weights.reshape(pair_total)
    ordering = jnp.argsort(pair_expert, stable=True)
    sorted_token = pair_token[ordering]
    sorted_gate = pair_gate[ordering]
    expert_ids = jnp.arange(EXPERTS).astype(jnp.int32)
    starts = lax.optimization_barrier(jnp.sum((pair_expert[None, :] < expert_ids[:, None]).astype(jnp.int32), axis=1))
    finishes = starts + lax.optimization_barrier(jnp.sum((pair_expert[None, :] == expert_ids[:, None]).astype(jnp.int32), axis=1))
    window = TOKENS // TOKENS_PER_UNIT * MOST
    offsets = jnp.arange(window).astype(jnp.int32)
    slice_width = HID // N_TP

    def one_expert(total, inputs):
        weight_in, weight_out, start, finish = inputs
        position = start + offsets
        inside = position < finish
        clipped = jnp.minimum(position, pair_total - 1)
        token_matrix_rows = sorted_token[clipped]
        gathered = normalized_input[token_matrix_rows]
        gate_up = jnp.dot(gathered, weight_in.reshape(D, 2 * HID), preferred_element_type=jnp.float32)
        activated = (jax.nn.silu(gate_up[:, :HID]) * gate_up[:, HID:]).astype(jnp.bfloat16)
        pieces = jnp.einsum('wsk,skd->wsd', activated.reshape(window, N_TP, slice_width).astype(jnp.float32), weight_out.reshape(N_TP, slice_width, D).astype(jnp.float32)).astype(jnp.bfloat16)
        expert_value = lax.optimization_barrier(jnp.sum(pieces.astype(jnp.float32), axis=1))
        factor = jnp.where(inside, sorted_gate[clipped], jnp.zeros_like(sorted_gate[clipped]))
        return (total.at[token_matrix_rows].add(expert_value * factor[:, None]), None)
    total, _ = lax.scan(one_expert, jnp.zeros((TOKENS, D), jnp.float32), (expert_in, expert_out, starts, finishes))
    return total

def reference(hidden_in, queries, latent_cache, lengths, w_uv, attn_weight, norm_gain, router, routes, live_counts, expert_in, expert_out):
    query_all = queries.reshape(TOKENS, HEADS, QK_DIM).astype(jnp.float32)
    cache_all = latent_cache.astype(jnp.float32)
    scores = jnp.einsum('jhr,jpr->jhp', query_all, cache_all) * score_scale
    positions = jnp.arange(CACHE_LEN).astype(jnp.int32)
    visible = positions[None, None, :] < lengths[:, None, None]
    scores = jnp.where(visible, scores, jnp.full_like(scores, -1e+30))
    highest = lax.optimization_barrier(jnp.max(scores, axis=2, keepdims=True))
    raised = jnp.exp(scores - highest)
    softmax_weights = (raised / lax.optimization_barrier(jnp.sum(raised, axis=2, keepdims=True))).astype(jnp.bfloat16)
    latent_out = jnp.einsum('jhp,jpc->jhc', softmax_weights.astype(jnp.float32), cache_all[:, :, :KV_RANK]).astype(jnp.bfloat16)
    up_proj = w_uv.reshape(HEADS, KV_RANK, V_DIM).astype(jnp.float32)
    head_out = jnp.einsum('jhc,hcv->jhv', latent_out.astype(jnp.float32), up_proj).astype(jnp.bfloat16)
    attention = jnp.dot(head_out.reshape(TOKENS, HEADS * V_DIM), attn_weight.reshape(HEADS * V_DIM, D), preferred_element_type=jnp.float32).astype(jnp.bfloat16)
    residual = hidden_in.astype(jnp.float32) + attention.astype(jnp.float32)
    normalized_input = (residual * lax.rsqrt(lax.optimization_barrier(jnp.mean(residual * residual, axis=1, keepdims=True)) + 1e-06) * norm_gain).astype(jnp.bfloat16)
    affinity = jax.nn.sigmoid(jnp.dot(normalized_input, router, preferred_element_type=jnp.float32))
    chosen = jnp.take_along_axis(affinity, routes, axis=1)
    token_ids = jnp.arange(TOKENS).astype(jnp.int32)
    living = (token_ids % TOKENS_PER_UNIT < live_counts[token_ids // TOKENS_PER_UNIT]).astype(jnp.float32)
    gate_weights = route_scale * chosen / lax.optimization_barrier(jnp.sum(chosen, axis=1, keepdims=True)) * living[:, None]
    expert_mix = routed_experts(normalized_input, routes, gate_weights, expert_in, expert_out)
    return (residual + expert_mix).astype(jnp.bfloat16)
```

```python
import jax
import jax.numpy as jnp
from jax import lax
from jax.sharding import Mesh
from jax.sharding import PartitionSpec as P

GRP = ("grp_0", "grp_1")
SEC_GRP = ("sec", "grp_0", "grp_1")
TP = ("x", "core")
GRP_TP = ("grp_0", "grp_1", "x", "core")
SEC_GRP_TP = ("sec", "grp_0", "grp_1", "x", "core")


score_scale = 192.0 ** (-0.5)
route_scale = 2.5


def gathered_by_axis(x, axes, dim):
    out = x
    for number in range(len(axes) - 1, -1, -1):
        out = lax.all_gather(out, axes[number], axis=dim, tiled=True)
    return out


def shifted(x, axis, step):
    size = lax.axis_size(axis)
    return lax.ppermute(x, axis, [(i, (i + step) % size) for i in range(size)])


def pair_of_blocks(blocks, chip, core):
    return jnp.stack(
        [
            lax.dynamic_index_in_dim(blocks, 2 * chip + core, 0, keepdims=False),
            lax.dynamic_index_in_dim(blocks, 2 * chip + 1 - core, 0, keepdims=False),
        ]
    )


def attention_rows(queries, latent_cache, lengths, w_uv):
    latent_width = w_uv.shape[2]
    query_block = queries[:, :, 0, :]
    scores = (
        jnp.einsum("bhr,bpr->bhp", query_block, latent_cache, preferred_element_type=jnp.float32)
        * score_scale
    )
    positions = jnp.arange(latent_cache.shape[1])
    visible = positions[None, None, :] < lengths[:, None, None]
    scores = jnp.where(visible, scores, -1e30)
    highest = jnp.max(scores, axis=2, keepdims=True)
    raised = jnp.exp(scores - highest)
    softmax_weights = (raised / jnp.sum(raised, axis=2, keepdims=True)).astype(jnp.bfloat16)
    latent_out = jnp.einsum(
        "bhp,bpc->bhc",
        softmax_weights,
        latent_cache[:, :, :latent_width],
        preferred_element_type=jnp.float32,
    ).astype(jnp.bfloat16)
    head_out = jnp.einsum(
        "bhc,hcv->bhv", latent_out, w_uv[:, 0], preferred_element_type=jnp.float32
    ).astype(jnp.bfloat16)
    return head_out.reshape(head_out.shape[0], -1)


def shards(
    hidden_in,
    queries,
    latent_cache,
    lengths,
    w_uv,
    attn_weight,
    norm_gain,
    router,
    routes,
    live_counts,
    expert_in,
    expert_out,
):
    count_of_tokens, width = hidden_in.shape
    groups = lax.axis_size(GRP)
    slices = lax.axis_size(TP)
    chips = lax.axis_size("x")
    chip, core = lax.axis_index("x"), lax.axis_index("core")
    part = width // slices
    slice_width = expert_in.shape[3]

    head_rows = attention_rows(queries, latent_cache, lengths, w_uv)
    head_rows, expert_in = lax.optimization_barrier((head_rows, expert_in))

    in_blocks = expert_in[0].reshape(slices, part, 2 * slice_width)
    in_slices = [
        shifted(pair_of_blocks(in_blocks, (chip + step) % chips, core), "x", step) if step else
        pair_of_blocks(in_blocks, chip, core)
        for step in range(chips)
    ]

    out_block = attn_weight[:, 0].reshape(-1, attn_weight.shape[3])
    partial_value = jnp.dot(
        gathered_by_axis(head_rows, GRP, 0), out_block, preferred_element_type=jnp.float32
    ).astype(jnp.bfloat16)
    partial_value = partial_value.reshape(groups * slices, count_of_tokens, -1)
    partial_value, expert_out = lax.optimization_barrier((partial_value, expert_out))
    arrived = lax.all_to_all(partial_value, GRP_TP, split_axis=0, concat_axis=0, tiled=True)
    summed = arrived.reshape(groups, slices, count_of_tokens, -1).astype(jnp.float32).sum(axis=1)
    attention = jnp.moveaxis(summed.astype(jnp.bfloat16), 0, 1).reshape(count_of_tokens, width)

    out_blocks = jnp.moveaxis(expert_out[0].reshape(slice_width, slices, part), 1, 0)
    out_pairs = [
        shifted(pair_of_blocks(out_blocks, (chip + step) % chips, core), "x", step) if step else
        pair_of_blocks(out_blocks, chip, core)
        for step in range(chips)
    ]
    out_own = jnp.concatenate([pair[0] for pair in out_pairs], axis=0)
    out_other = shifted(jnp.concatenate([pair[1] for pair in out_pairs], axis=0), "core", 1)

    residual = hidden_in.astype(jnp.float32) + attention.astype(jnp.float32)
    normalized_input = (
        residual
        * lax.rsqrt(jnp.mean(residual * residual, axis=1, keepdims=True) + 1e-06)
        * norm_gain
    ).astype(jnp.bfloat16)
    experts = router.shape[1]
    per_token = routes.shape[1]
    capacity = max(2, 2 * count_of_tokens * per_token // experts)
    affinity = jax.nn.sigmoid(jnp.dot(normalized_input, router, preferred_element_type=jnp.float32))
    picked = routes[:, :, None] == jnp.arange(experts)[None, None, :]
    chosen = jnp.sum(jnp.where(picked, affinity[:, None, :], 0.0), axis=2)
    living = jnp.arange(count_of_tokens) < live_counts[0]
    gate_weights = (
        route_scale
        * chosen
        / jnp.sum(chosen, axis=1, keepdims=True)
        * living[:, None].astype(jnp.float32)
    )
    routed = jnp.any(picked, axis=1) & living[:, None]
    routed_count = routed.astype(jnp.int32)
    slot_index = jnp.cumsum(routed_count, axis=0) - routed_count
    placed_tokens = routed[:, :, None] & (
        slot_index[:, :, None] == jnp.arange(capacity)[None, None, :]
    )
    expert_gate = jnp.sum(jnp.where(picked, gate_weights[:, :, None], 0.0), axis=1)
    outgoing = jnp.einsum(
        "poy,ptj->otyj",
        placed_tokens.astype(jnp.bfloat16),
        normalized_input.reshape(count_of_tokens, slices, part),
        preferred_element_type=jnp.float32,
    ).astype(jnp.bfloat16)
    combine_rows = placed_tokens.astype(jnp.float32) * expert_gate[:, :, None]

    rows = lax.all_to_all(
        outgoing.reshape(experts * slices, capacity, part),
        SEC_GRP_TP, split_axis=0, concat_axis=0, tiled=True,
    ).reshape(-1, part)
    other_rows = shifted(rows, "core", 1)
    gate_up = None
    for step in (2, 1, 3, 0):
        block = jnp.dot(rows, in_slices[step][0], preferred_element_type=jnp.float32) + jnp.dot(
            other_rows, in_slices[step][1], preferred_element_type=jnp.float32
        )
        if step:
            block = shifted(block.astype(jnp.bfloat16), "x", -step).astype(jnp.float32)
        gate_up = block if gate_up is None else gate_up + block
    activated = (jax.nn.silu(gate_up[:, :slice_width]) * gate_up[:, slice_width:]).astype(
        jnp.bfloat16
    )
    hidden_own = jnp.concatenate(
        [activated] + [shifted(activated, "x", step) for step in range(1, chips)], axis=1
    )
    hidden_other = shifted(hidden_own, "core", 1)
    values = (
        jnp.dot(hidden_own, out_own, preferred_element_type=jnp.float32)
        + jnp.dot(hidden_other, out_other, preferred_element_type=jnp.float32)
    ).astype(jnp.bfloat16)
    back = lax.all_to_all(
        values.reshape(experts * slices, capacity, part),
        SEC_GRP_TP, split_axis=0, concat_axis=0, tiled=True,
    ).reshape(experts, slices, capacity, part)
    coarse = lax.reduce_precision(combine_rows, 8, 7)
    weights = jnp.concatenate([coarse, combine_rows - coarse], axis=0).astype(jnp.bfloat16)
    mixed = jnp.einsum("poy,otyj->ptj", weights, back, preferred_element_type=jnp.float32)
    expert_mix = (mixed[:count_of_tokens] + mixed[count_of_tokens:]).reshape(count_of_tokens, width)
    return (residual + expert_mix).astype(jnp.bfloat16)


def solution(mesh):
    torus = Mesh(
        mesh.devices.reshape(mesh.shape["sec"], 8, 2, mesh.shape["tp"] // 2, 2), SEC_GRP_TP
    )
    in_specs = (
        P(SEC_GRP_TP, None),
        P(SEC_GRP, None, TP, None),
        P(SEC_GRP, None, None),
        P(SEC_GRP),
        P(None, TP, None, None),
        P(None, TP, None, GRP),
        P(),
        P(),
        P(SEC_GRP_TP, None),
        P(SEC_GRP_TP),
        P(SEC_GRP, None, None, TP),
        P(SEC_GRP, TP, None),
    )
    out_specs = P(SEC_GRP_TP, None)
    return jax.shard_map(
        shards, mesh=torus, in_specs=in_specs, out_specs=out_specs, check_vma=False
    )
```

```python
import jax
import jax.numpy as jnp
from jax import lax
from jax.sharding import Mesh
from jax.sharding import PartitionSpec as P

GRP = ("grp_0", "grp_1")
SEC_GRP = ("sec", "grp_0", "grp_1")
TP = ("x", "core")
GRP_TP = ("grp_0", "grp_1", "x", "core")
SEC_GRP_TP = ("sec", "grp_0", "grp_1", "x", "core")


score_scale = 192.0 ** (-0.5)
route_scale = 2.5


def gathered_by_axis(x, axes, dim):
    out = x
    for number in range(len(axes) - 1, -1, -1):
        out = lax.all_gather(out, axes[number], axis=dim, tiled=True)
    return out


def shifted(x, axis, step):
    size = lax.axis_size(axis)
    return lax.ppermute(x, axis, [(i, (i + step) % size) for i in range(size)])


def halves(blocks, core, size, dim):
    return [lax.dynamic_slice_in_dim(blocks, number * size, size, dim) for number in (core, 1 - core)]


def in_width_slices(expert_in, chips, chip, core):
    width, _, slice_width = expert_in.shape
    rows = width // chips
    parts = []
    for step in range(chips):
        part = lax.dynamic_slice_in_dim(expert_in, (chip + step) % chips * rows, rows, 0)
        if step:
            part = shifted(part, "x", step)
        parts.append(halves(part.reshape(rows, 2 * slice_width), core, rows // 2, 0))
    return [jnp.concatenate(side, axis=1) for side in zip(*parts)]


def out_width_slices(expert_out, chips, chip, core):
    columns = expert_out.shape[1] // chips
    parts = []
    for step in range(chips):
        part = lax.dynamic_slice_in_dim(expert_out, (chip + step) % chips * columns, columns, 1)
        if step:
            part = shifted(part, "x", step)
        parts.append(part)
    own, other = halves(jnp.concatenate(parts, axis=0), core, columns // 2, 1)
    return own, shifted(other, "core", 1)


def attention_rows(queries, latent_cache, lengths, w_uv):
    latent_width = w_uv.shape[2]
    query_block = queries[:, :, 0, :]
    scores = (
        jnp.einsum("bhr,bpr->bhp", query_block, latent_cache, preferred_element_type=jnp.float32)
        * score_scale
    )
    positions = jnp.arange(latent_cache.shape[1])
    visible = positions[None, None, :] < lengths[:, None, None]
    scores = jnp.where(visible, scores, -1e30)
    highest = jnp.max(scores, axis=2, keepdims=True)
    raised = jnp.exp(scores - highest)
    softmax_weights = (raised / jnp.sum(raised, axis=2, keepdims=True)).astype(jnp.bfloat16)
    latent_out = jnp.einsum(
        "bhp,bpc->bhc",
        softmax_weights,
        latent_cache[:, :, :latent_width],
        preferred_element_type=jnp.float32,
    ).astype(jnp.bfloat16)
    head_out = jnp.einsum(
        "bhc,hcv->bhv", latent_out, w_uv[:, 0], preferred_element_type=jnp.float32
    ).astype(jnp.bfloat16)
    return head_out.reshape(head_out.shape[0], -1)


def shards(
    hidden_in,
    queries,
    latent_cache,
    lengths,
    w_uv,
    attn_weight,
    norm_gain,
    router,
    routes,
    live_counts,
    expert_in,
    expert_out,
):
    count_of_tokens, width = hidden_in.shape
    groups = lax.axis_size(GRP)
    slices = lax.axis_size(TP)
    chips = lax.axis_size("x")
    chip, core = lax.axis_index("x"), lax.axis_index("core")
    part = width // slices
    slice_width = expert_in.shape[3]

    head_rows = attention_rows(queries, latent_cache, lengths, w_uv)
    head_rows, expert_in = lax.optimization_barrier((head_rows, expert_in))

    in_own, in_other = in_width_slices(expert_in[0], chips, chip, core)

    out_block = attn_weight[:, 0].reshape(-1, attn_weight.shape[3])
    partial_value = jnp.dot(
        gathered_by_axis(head_rows, GRP, 0), out_block, preferred_element_type=jnp.float32
    ).astype(jnp.bfloat16)
    partial_value = partial_value.reshape(groups * slices, count_of_tokens, -1)
    partial_value, expert_out, in_own, in_other = lax.optimization_barrier(
        (partial_value, expert_out, in_own, in_other)
    )
    arrived = lax.all_to_all(partial_value, GRP_TP, split_axis=0, concat_axis=0, tiled=True)
    summed = arrived.reshape(groups, slices, count_of_tokens, -1).astype(jnp.float32).sum(axis=1)
    attention = jnp.moveaxis(summed.astype(jnp.bfloat16), 0, 1).reshape(count_of_tokens, width)

    out_own, out_other = out_width_slices(expert_out[0], chips, chip, core)
    attention, out_own, out_other = lax.optimization_barrier((attention, out_own, out_other))

    residual = hidden_in.astype(jnp.float32) + attention.astype(jnp.float32)
    normalized_input = (
        residual
        * lax.rsqrt(jnp.mean(residual * residual, axis=1, keepdims=True) + 1e-06)
        * norm_gain
    ).astype(jnp.bfloat16)
    experts = router.shape[1]
    per_token = routes.shape[1]
    capacity = max(2, 2 * count_of_tokens * per_token // experts)
    affinity = jax.nn.sigmoid(jnp.dot(normalized_input, router, preferred_element_type=jnp.float32))
    picked = routes[:, :, None] == jnp.arange(experts)[None, None, :]
    chosen = jnp.sum(jnp.where(picked, affinity[:, None, :], 0.0), axis=2)
    living = jnp.arange(count_of_tokens) < live_counts[0]
    gate_weights = (
        route_scale
        * chosen
        / jnp.sum(chosen, axis=1, keepdims=True)
        * living[:, None].astype(jnp.float32)
    )
    routed = jnp.any(picked, axis=1) & living[:, None]
    routed_count = routed.astype(jnp.int32)
    slot_index = jnp.cumsum(routed_count, axis=0) - routed_count
    placed_tokens = routed[:, :, None] & (
        slot_index[:, :, None] == jnp.arange(capacity)[None, None, :]
    )
    expert_gate = jnp.sum(jnp.where(picked, gate_weights[:, :, None], 0.0), axis=1)
    outgoing = jnp.einsum(
        "poy,ptj->otyj",
        placed_tokens.astype(jnp.bfloat16),
        normalized_input.reshape(count_of_tokens, slices, part),
        preferred_element_type=jnp.float32,
    ).astype(jnp.bfloat16)
    combine_rows = placed_tokens.astype(jnp.float32) * expert_gate[:, :, None]

    rows = lax.all_to_all(
        outgoing.reshape(experts * slices, capacity, part),
        SEC_GRP_TP, split_axis=0, concat_axis=0, tiled=True,
    ).reshape(-1, part)
    other_rows = shifted(rows, "core", 1)
    products = jnp.dot(rows, in_own, preferred_element_type=jnp.float32) + jnp.dot(
        other_rows, in_other, preferred_element_type=jnp.float32
    )
    products = jnp.split(products, chips, axis=1)
    gate_up = products[0]
    for step in (2, 1, 3):
        block = shifted(products[step].astype(jnp.bfloat16), "x", -step)
        gate_up = gate_up + block.astype(jnp.float32)
    activated = (jax.nn.silu(gate_up[:, :slice_width]) * gate_up[:, slice_width:]).astype(
        jnp.bfloat16
    )
    hidden_own = jnp.concatenate(
        [activated] + [shifted(activated, "x", step) for step in range(1, chips)], axis=1
    )
    hidden_other = shifted(hidden_own, "core", 1)
    values = (
        jnp.dot(hidden_own, out_own, preferred_element_type=jnp.float32)
        + jnp.dot(hidden_other, out_other, preferred_element_type=jnp.float32)
    ).astype(jnp.bfloat16)
    back = lax.all_to_all(
        values.reshape(experts * slices, capacity, part),
        SEC_GRP_TP, split_axis=0, concat_axis=0, tiled=True,
    ).reshape(experts, slices, capacity, part)
    coarse = lax.reduce_precision(combine_rows, 8, 7)
    weights = jnp.concatenate([coarse, combine_rows - coarse], axis=0).astype(jnp.bfloat16)
    mixed = jnp.einsum("poy,otyj->ptj", weights, back, preferred_element_type=jnp.float32)
    expert_mix = (mixed[:count_of_tokens] + mixed[count_of_tokens:]).reshape(count_of_tokens, width)
    return (residual + expert_mix).astype(jnp.bfloat16)


def solution(mesh):
    torus = Mesh(
        mesh.devices.reshape(mesh.shape["sec"], 8, 2, mesh.shape["tp"] // 2, 2), SEC_GRP_TP
    )
    in_specs = (
        P(SEC_GRP_TP, None),
        P(SEC_GRP, None, TP, None),
        P(SEC_GRP, None, None),
        P(SEC_GRP),
        P(None, TP, None, None),
        P(None, TP, None, GRP),
        P(),
        P(),
        P(SEC_GRP_TP, None),
        P(SEC_GRP_TP),
        P(SEC_GRP, None, None, TP),
        P(SEC_GRP, TP, None),
    )
    out_specs = P(SEC_GRP_TP, None)
    return jax.shard_map(
        shards, mesh=torus, in_specs=in_specs, out_specs=out_specs, check_vma=False
    )
```

```python
import jax
import jax.numpy as jnp
from jax import lax
from jax.sharding import Mesh
from jax.sharding import PartitionSpec as P


GRP = ("grp_0", "grp_1")
SEC_GRP = ("sec", "grp_0", "grp_1")
TP = ("x", "core")
GRP_TP = ("grp_0", "grp_1", "x", "core")
SEC_GRP_TP = ("sec", "grp_0", "grp_1", "x", "core")


score_scale = 192.0 ** (-0.5)
route_scale = 2.5


def shifted(x, axis, step):
    size = lax.axis_size(axis)
    return lax.ppermute(x, axis, [(i, (i + step) % size) for i in range(size)])


def rolled(blocks, count):
    size = blocks.shape[0]
    return lax.dynamic_slice_in_dim(jnp.concatenate([blocks, blocks]), size - count, size, 0)


def around_the_ring(block):
    middle = block.shape[0] // 2
    before = {step: shifted(block, "grp_0", step) for step in (1, 2)}
    after = {step: shifted(block, "grp_0", -step) for step in (1, 2)}
    before[3] = shifted(before[2], "grp_0", 1)
    after[3] = shifted(after[2], "grp_0", -1)
    far = jnp.concatenate(
        [shifted(before[2][:middle], "grp_0", 2), shifted(after[2][middle:], "grp_0", -2)]
    )
    near = [block, after[1], after[2], before[2], before[1]]
    return near, [after[3], far, before[3]]


def projected(head_rows, out_block):
    rows, columns = head_rows.shape[0], out_block.shape[1]
    partner = shifted(head_rows, "grp_1", 1)
    products = []
    for gathered in zip(around_the_ring(head_rows), around_the_ring(partner)):
        product = jnp.dot(
            jnp.concatenate(gathered[0] + gathered[1]), out_block, preferred_element_type=jnp.float32
        ).astype(jnp.bfloat16)
        products.append(product.reshape(2, len(gathered[0]), rows, columns))
    near, far = products
    places = jnp.concatenate([near[:, :3], far, near[:, 3:]], axis=1)
    places = rolled(places, lax.axis_index("grp_1"))
    return rolled(jnp.moveaxis(places, 1, 0), lax.axis_index("grp_0"))


def halves(blocks, core, size, dim):
    return [lax.dynamic_slice_in_dim(blocks, number * size, size, dim) for number in (core, 1 - core)]


def in_width_slices(expert_in, chips, chip, core):
    width, _, slice_width = expert_in.shape
    rows = width // chips
    parts = []
    for step in range(chips):
        part = lax.dynamic_slice_in_dim(expert_in, (chip + step) % chips * rows, rows, 0)
        if step:
            part = shifted(part, "x", step)
        parts.append(halves(part.reshape(rows, 2 * slice_width), core, rows // 2, 0))
    return [jnp.concatenate(side, axis=1) for side in zip(*parts)]


def out_width_slices(expert_out, chips, chip, core):
    columns = expert_out.shape[1] // chips
    parts = []
    for step in range(chips):
        part = lax.dynamic_slice_in_dim(expert_out, (chip + step) % chips * columns, columns, 1)
        if step:
            part = shifted(part, "x", step)
        parts.append(part)
    own, other = halves(jnp.concatenate(parts, axis=0), core, columns // 2, 1)
    return own, shifted(other, "core", 1)


def attention_rows(queries, latent_cache, lengths, w_uv):
    latent_width = w_uv.shape[2]
    query_block = queries[:, :, 0, :]
    scores = (
        jnp.einsum("bhr,bpr->bhp", query_block, latent_cache, preferred_element_type=jnp.float32)
        * score_scale
    )
    positions = jnp.arange(latent_cache.shape[1])
    visible = positions[None, None, :] < lengths[:, None, None]
    scores = jnp.where(visible, scores, -1e30)
    highest = jnp.max(scores, axis=2, keepdims=True)
    raised = jnp.exp(scores - highest)
    softmax_weights = (raised / jnp.sum(raised, axis=2, keepdims=True)).astype(jnp.bfloat16)
    latent_out = jnp.einsum(
        "bhp,bpc->bhc",
        softmax_weights,
        latent_cache[:, :, :latent_width],
        preferred_element_type=jnp.float32,
    ).astype(jnp.bfloat16)
    head_out = jnp.einsum(
        "bhc,hcv->bhv", latent_out, w_uv[:, 0], preferred_element_type=jnp.float32
    ).astype(jnp.bfloat16)
    return head_out.reshape(head_out.shape[0], -1)


def layer(
    hidden_in,
    queries,
    latent_cache,
    lengths,
    w_uv,
    attn_weight,
    norm_gain,
    router,
    routes,
    live_counts,
    expert_in,
    expert_out,
):
    count_of_tokens, width = hidden_in.shape
    groups = lax.axis_size(GRP)
    slices = lax.axis_size(TP)
    chips = lax.axis_size("x")
    chip, core = lax.axis_index("x"), lax.axis_index("core")
    part = width // slices
    slice_width = expert_in.shape[3]

    head_rows = attention_rows(queries, latent_cache, lengths, w_uv)
    head_rows, expert_in, expert_out = lax.optimization_barrier(
        (head_rows, expert_in, expert_out)
    )

    in_own, in_other = in_width_slices(expert_in[0], chips, chip, core)

    out_block = attn_weight[:, 0].reshape(-1, attn_weight.shape[3])
    partial_value = projected(head_rows, out_block)
    partial_value = partial_value.reshape(groups * slices, count_of_tokens, -1)
    arrived = lax.all_to_all(partial_value, GRP_TP, split_axis=0, concat_axis=0, tiled=True)
    summed = arrived.reshape(groups, slices, count_of_tokens, -1).astype(jnp.float32).sum(axis=1)
    attention = jnp.moveaxis(summed.astype(jnp.bfloat16), 0, 1).reshape(count_of_tokens, width)

    out_own, out_other = out_width_slices(expert_out[0], chips, chip, core)
    attention, in_own, in_other, out_own, out_other = lax.optimization_barrier(
        (attention, in_own, in_other, out_own, out_other)
    )

    residual = hidden_in.astype(jnp.float32) + attention.astype(jnp.float32)
    normalized_input = (
        residual
        * lax.rsqrt(jnp.mean(residual * residual, axis=1, keepdims=True) + 1e-06)
        * norm_gain
    ).astype(jnp.bfloat16)
    experts = router.shape[1]
    per_token = routes.shape[1]
    capacity = max(2, 2 * count_of_tokens * per_token // experts)
    affinity = jax.nn.sigmoid(jnp.dot(normalized_input, router, preferred_element_type=jnp.float32))
    picked = routes[:, :, None] == jnp.arange(experts)[None, None, :]
    chosen = jnp.sum(jnp.where(picked, affinity[:, None, :], 0.0), axis=2)
    living = jnp.arange(count_of_tokens) < live_counts[0]
    gate_weights = (
        route_scale
        * chosen
        / jnp.sum(chosen, axis=1, keepdims=True)
        * living[:, None].astype(jnp.float32)
    )
    routed = jnp.any(picked, axis=1) & living[:, None]
    routed_count = routed.astype(jnp.int32)
    slot_index = jnp.cumsum(routed_count, axis=0) - routed_count
    placed_tokens = routed[:, :, None] & (
        slot_index[:, :, None] == jnp.arange(capacity)[None, None, :]
    )
    expert_gate = jnp.sum(jnp.where(picked, gate_weights[:, :, None], 0.0), axis=1)
    outgoing = jnp.einsum(
        "poy,ptj->otyj",
        placed_tokens.astype(jnp.bfloat16),
        normalized_input.reshape(count_of_tokens, slices, part),
        preferred_element_type=jnp.float32,
    ).astype(jnp.bfloat16)
    combine_rows = placed_tokens.astype(jnp.float32) * expert_gate[:, :, None]

    rows = lax.all_to_all(
        outgoing.reshape(experts * slices, capacity, part),
        SEC_GRP_TP, split_axis=0, concat_axis=0, tiled=True,
    ).reshape(-1, part)
    other_rows = shifted(rows, "core", 1)
    products = jnp.dot(rows, in_own, preferred_element_type=jnp.float32) + jnp.dot(
        other_rows, in_other, preferred_element_type=jnp.float32
    )
    products = jnp.split(products, chips, axis=1)
    gate_up = products[0]
    for step in (2, 1, 3):
        block = shifted(products[step].astype(jnp.bfloat16), "x", -step)
        gate_up = gate_up + block.astype(jnp.float32)
    activated = (jax.nn.silu(gate_up[:, :slice_width]) * gate_up[:, slice_width:]).astype(
        jnp.bfloat16
    )
    hidden_own = jnp.concatenate(
        [activated] + [shifted(activated, "x", step) for step in range(1, chips)], axis=1
    )
    hidden_other = shifted(hidden_own, "core", 1)
    values = (
        jnp.dot(hidden_own, out_own, preferred_element_type=jnp.float32)
        + jnp.dot(hidden_other, out_other, preferred_element_type=jnp.float32)
    ).astype(jnp.bfloat16)
    back = lax.all_to_all(
        values.reshape(experts * slices, capacity, part),
        SEC_GRP_TP, split_axis=0, concat_axis=0, tiled=True,
    ).reshape(experts, slices, capacity, part)
    coarse = lax.reduce_precision(combine_rows, 8, 7)
    weights = jnp.concatenate([coarse, combine_rows - coarse], axis=0).astype(jnp.bfloat16)
    mixed = jnp.einsum("poy,otyj->ptj", weights, back, preferred_element_type=jnp.float32)
    expert_mix = (mixed[:count_of_tokens] + mixed[count_of_tokens:]).reshape(count_of_tokens, width)
    return (residual + expert_mix).astype(jnp.bfloat16)


def solution(mesh):
    torus = Mesh(
        mesh.devices.reshape(mesh.shape["sec"], 8, 2, mesh.shape["tp"] // 2, 2), SEC_GRP_TP
    )
    in_specs = (
        P(SEC_GRP_TP, None),
        P(SEC_GRP, None, TP, None),
        P(SEC_GRP, None, None),
        P(SEC_GRP),
        P(None, TP, None, None),
        P(None, TP, None, GRP),
        P(),
        P(),
        P(SEC_GRP_TP, None),
        P(SEC_GRP_TP),
        P(SEC_GRP, None, None, TP),
        P(SEC_GRP, TP, None),
    )
    out_specs = P(SEC_GRP_TP, None)
    return jax.shard_map(layer, mesh=torus, in_specs=in_specs, out_specs=out_specs, check_vma=False)
```

```python
import jax
import jax.numpy as jnp
from jax import lax
from jax.sharding import Mesh
from jax.sharding import PartitionSpec as P


GRP = ("grp_0", "grp_1")
SEC_GRP = ("sec", "grp_0", "grp_1")
TP = ("x", "core")
GRP_TP = ("grp_0", "grp_1", "x", "core")
TP_SEC_GRP = ("x", "core", "sec", "grp_0", "grp_1")
SEC_GRP_TP = ("sec", "grp_0", "grp_1", "x", "core")


score_scale = 192.0 ** (-0.5)
route_scale = 2.5


def shifted(x, axis, step):
    size = lax.axis_size(axis)
    return lax.ppermute(x, axis, [(i, (i + step) % size) for i in range(size)])


def rolled(blocks, count):
    size = blocks.shape[0]
    return lax.dynamic_slice_in_dim(jnp.concatenate([blocks, blocks]), size - count, size, 0)


def around_the_ring(block):
    middle = block.shape[0] // 2
    before = {step: shifted(block, "grp_0", step) for step in (1, 2)}
    after = {step: shifted(block, "grp_0", -step) for step in (1, 2)}
    before[3] = shifted(before[2], "grp_0", 1)
    after[3] = shifted(after[2], "grp_0", -1)
    far = jnp.concatenate(
        [shifted(before[2][:middle], "grp_0", 2), shifted(after[2][middle:], "grp_0", -2)]
    )
    near = [block, after[1], after[2], before[2], before[1]]
    return near, [after[3], far, before[3]]


def projected(head_rows, out_block):
    rows, columns = head_rows.shape[0], out_block.shape[1]
    partner = shifted(head_rows, "grp_1", 1)
    products = []
    for gathered in zip(around_the_ring(head_rows), around_the_ring(partner)):
        product = jnp.dot(
            jnp.concatenate(gathered[0] + gathered[1]), out_block, preferred_element_type=jnp.float32
        ).astype(jnp.bfloat16)
        products.append(product.reshape(2, len(gathered[0]), rows, columns))
    near, far = products
    places = jnp.concatenate([near[:, :3], far, near[:, 3:]], axis=1)
    places = rolled(places, lax.axis_index("grp_1"))
    return rolled(jnp.moveaxis(places, 1, 0), lax.axis_index("grp_0"))


def rolled(blocks, count):
    size = blocks.shape[0]
    return lax.dynamic_slice_in_dim(jnp.concatenate([blocks, blocks]), size - count, size, 0)


def own_and_other(array, core, dim):
    size = array.shape[dim] // 2
    return [lax.dynamic_slice_in_dim(array, number * size, size, dim) for number in (core, 1 - core)]


def around_the_ring(block):
    middle = block.shape[0] // 2
    before = {step: shifted(block, "grp_0", step) for step in (2, 1)}
    after = {step: shifted(block, "grp_0", -step) for step in (2, 1)}
    before[3] = shifted(before[2], "grp_0", 1)
    after[3] = shifted(after[2], "grp_0", -1)
    opposite = jnp.concatenate(
        [shifted(before[2][:middle], "grp_0", 2), shifted(after[2][middle:], "grp_0", -2)]
    )
    return [block, after[1], after[2], before[2], before[1]], [after[3], opposite, before[3]]


def projected(head_rows, out_block):
    rows, columns = head_rows.shape[0], out_block.shape[1]
    partner = shifted(head_rows, "grp_1", 1)
    products = []
    for gathered in around_the_ring(jnp.concatenate([head_rows, partner])):
        product = jnp.dot(
            jnp.concatenate(gathered), out_block, preferred_element_type=jnp.float32
        ).astype(jnp.bfloat16)
        products.append(product.reshape(len(gathered), 2, rows, columns))
    near, far = products
    places = jnp.concatenate([near[:3], far, near[3:]])
    places = rolled(jnp.moveaxis(places, 1, 0), lax.axis_index("grp_1"))
    return rolled(jnp.moveaxis(places, 0, 1), lax.axis_index("grp_0"))


def attention_rows(queries, latent_cache, lengths, w_uv):
    latent_width = w_uv.shape[2]
    query_block = queries[:, :, 0, :]
    scores = (
        jnp.einsum("bhr,bpr->bhp", query_block, latent_cache, preferred_element_type=jnp.float32)
        * score_scale
    )
    positions = jnp.arange(latent_cache.shape[1])
    visible = positions[None, None, :] < lengths[:, None, None]
    scores = jnp.where(visible, scores, -1e30)
    highest = jnp.max(scores, axis=2, keepdims=True)
    raised = jnp.exp(scores - highest)
    softmax_weights = (raised / jnp.sum(raised, axis=2, keepdims=True)).astype(jnp.bfloat16)
    latent_out = jnp.einsum(
        "bhp,bpc->bhc",
        softmax_weights,
        latent_cache[:, :, :latent_width],
        preferred_element_type=jnp.float32,
    ).astype(jnp.bfloat16)
    head_out = jnp.einsum(
        "bhc,hcv->bhv", latent_out, w_uv[:, 0], preferred_element_type=jnp.float32
    ).astype(jnp.bfloat16)
    return head_out.reshape(head_out.shape[0], -1)


def layer(
    hidden_in,
    queries,
    latent_cache,
    lengths,
    w_uv,
    attn_weight,
    norm_gain,
    router,
    routes,
    live_counts,
    expert_in,
    expert_out,
):
    count_of_tokens, width = hidden_in.shape
    groups = lax.axis_size(GRP)
    slices = lax.axis_size(TP)
    chips = lax.axis_size("x")
    chip, core = lax.axis_index("x"), lax.axis_index("core")
    part = width // slices
    slice_width = expert_in.shape[3]

    head_rows = attention_rows(queries, latent_cache, lengths, w_uv)
    head_rows, expert_in, expert_out = lax.optimization_barrier(
        (head_rows, expert_in, expert_out)
    )

    rows_of_chip = width // chips
    in_parts = [
        lax.dynamic_slice_in_dim(expert_in[0], (chip - step) % chips * rows_of_chip, rows_of_chip, 0)
        for step in range(chips)
    ]
    in_parts[1:] = [shifted(in_parts[step], "x", -step) for step in range(1, chips)]
    out_before, out_after = shifted(expert_out[0], "x", 1), shifted(expert_out[0], "x", -1)

    out_block = attn_weight[:, 0].reshape(-1, attn_weight.shape[3])
    partial_value = projected(head_rows, out_block)
    partial_value = partial_value.reshape(groups * slices, count_of_tokens, -1)
    arrived = lax.all_to_all(partial_value, GRP_TP, split_axis=0, concat_axis=0, tiled=True)
    summed = arrived.reshape(groups, slices, count_of_tokens, -1).astype(jnp.float32).sum(axis=1)
    attention = jnp.moveaxis(summed.astype(jnp.bfloat16), 0, 1).reshape(count_of_tokens, width)

    residual = hidden_in.astype(jnp.float32) + attention.astype(jnp.float32)
    normalized_input = (
        residual
        * lax.rsqrt(jnp.mean(residual * residual, axis=1, keepdims=True) + 1e-06)
        * norm_gain
    ).astype(jnp.bfloat16)
    experts = router.shape[1]
    per_token = routes.shape[1]
    capacity = max(2, 2 * count_of_tokens * per_token // experts)
    affinity = jax.nn.sigmoid(jnp.dot(normalized_input, router, preferred_element_type=jnp.float32))
    picked = routes[:, :, None] == jnp.arange(experts)[None, None, :]
    chosen = jnp.sum(jnp.where(picked, affinity[:, None, :], 0.0), axis=2)
    living = jnp.arange(count_of_tokens) < live_counts[0]
    gate_weights = (
        route_scale
        * chosen
        / jnp.sum(chosen, axis=1, keepdims=True)
        * living[:, None].astype(jnp.float32)
    )
    routed = jnp.any(picked, axis=1) & living[:, None]
    routed_count = routed.astype(jnp.int32)
    slot_index = jnp.cumsum(routed_count, axis=0) - routed_count
    placed_tokens = routed[:, :, None] & (
        slot_index[:, :, None] == jnp.arange(capacity)[None, None, :]
    )
    expert_gate = jnp.sum(jnp.where(picked, gate_weights[:, :, None], 0.0), axis=1)
    outgoing = jnp.einsum(
        "poy,ptj->toyj",
        placed_tokens.astype(jnp.bfloat16),
        normalized_input.reshape(count_of_tokens, slices, part),
        preferred_element_type=jnp.float32,
    ).astype(jnp.bfloat16)
    combine_rows = placed_tokens.astype(jnp.float32) * expert_gate[:, :, None]
    outgoing = outgoing.reshape(slices * experts, capacity, part)
    rows = lax.all_to_all(
        outgoing, TP_SEC_GRP, split_axis=0, concat_axis=0, tiled=True
    ).reshape(-1, part)

    in_parts, out_before, out_after, _ = lax.optimization_barrier(
        (in_parts, out_before, out_after, outgoing)
    )
    in_columns = jnp.concatenate(
        [p.reshape(rows_of_chip, 2 * slice_width) for p in in_parts], axis=1
    )
    in_own, in_other = own_and_other(in_columns, core, 0)
    middle = slice_width // 2
    out_opposite = [
        shifted(out_before[:middle], "x", 1), shifted(out_after[middle:], "x", -1)
    ]
    out_own = jnp.concatenate([expert_out[0], out_after, *out_opposite, out_before])
    out_other = shifted(out_own, "core", 1)

    other_rows = shifted(rows, "core", 1)
    products = jnp.dot(rows, in_own, preferred_element_type=jnp.float32) + jnp.dot(
        other_rows, in_other, preferred_element_type=jnp.float32
    )
    gate_up = lax.all_to_all(
        products.astype(jnp.bfloat16).reshape(chips, -1, products.shape[1]),
        "x", split_axis=0, concat_axis=0, tiled=True,
    )
    parts_of = gate_up.astype(jnp.float32)
    activated = []
    for number in range(chips):
        starts = [(number - p) % chips * 2 * slice_width for p in range(chips)]
        gate_value, up_value = (
            sum(
                parts_of[p, :, start + first : start + first + slice_width]
                for p, start in enumerate(starts)
            )
            for first in (0, slice_width)
        )
        activated.append((jax.nn.silu(gate_value) * up_value).astype(jnp.bfloat16))
    activated = jnp.concatenate(list(rolled(jnp.stack(activated), chips - chip)), axis=1)
    hidden_own, hidden_sent = own_and_other(activated, core, 0)
    hidden_other = shifted(hidden_sent, "core", 1)
    values = (
        jnp.dot(hidden_own, out_own, preferred_element_type=jnp.float32)
        + jnp.dot(hidden_other, out_other, preferred_element_type=jnp.float32)
    ).astype(jnp.bfloat16)
    back = lax.all_to_all(
        values.reshape(experts, capacity, width), SEC_GRP, split_axis=0, concat_axis=0, tiled=True
    ).reshape(experts * capacity, width)
    coarse = lax.reduce_precision(combine_rows, 8, 7)
    weights = jnp.concatenate([coarse, combine_rows - coarse], axis=0).astype(jnp.bfloat16)
    mixed = jnp.dot(
        weights.reshape(2 * count_of_tokens, -1), back, preferred_element_type=jnp.float32
    )
    expert_mix = mixed[:count_of_tokens] + mixed[count_of_tokens:]
    return (residual + expert_mix).astype(jnp.bfloat16)


def solution(mesh):
    torus = Mesh(
        mesh.devices.reshape(mesh.shape["sec"], 8, 2, mesh.shape["tp"] // 2, 2), SEC_GRP_TP
    )
    in_specs = (
        P(SEC_GRP_TP, None),
        P(SEC_GRP, None, TP, None),
        P(SEC_GRP, None, None),
        P(SEC_GRP),
        P(None, TP, None, None),
        P(None, TP, None, GRP),
        P(),
        P(),
        P(SEC_GRP_TP, None),
        P(SEC_GRP_TP),
        P(SEC_GRP, None, None, TP),
        P(SEC_GRP, TP, None),
    )
    out_specs = P(SEC_GRP_TP, None)
    return jax.shard_map(layer, mesh=torus, in_specs=in_specs, out_specs=out_specs, check_vma=False)
```

```python
import jax
import jax.numpy as jnp
from jax import lax
from jax.sharding import Mesh
from jax.sharding import PartitionSpec as P


GRP = ("grp_0", "grp_1")
SEC_GRP = ("sec", "grp_0", "grp_1")
TP = ("x", "core")
GRP_TP = ("grp_0", "grp_1", "x", "core")
SEC_GRP_TP = ("sec", "grp_0", "grp_1", "x", "core")


score_scale = 192.0 ** (-0.5)
route_scale = 2.5


def shifted(x, axis, step):
    size = lax.axis_size(axis)
    return lax.ppermute(x, axis, [(i, (i + step) % size) for i in range(size)])


def rolled(blocks, count):
    size = blocks.shape[0]
    return lax.dynamic_slice_in_dim(jnp.concatenate([blocks, blocks]), size - count, size, 0)


def around_the_ring(block):
    middle = block.shape[0] // 2
    before = {step: shifted(block, "grp_0", step) for step in (1, 2)}
    after = {step: shifted(block, "grp_0", -step) for step in (1, 2)}
    before[3] = shifted(before[2], "grp_0", 1)
    after[3] = shifted(after[2], "grp_0", -1)
    far = jnp.concatenate(
        [shifted(before[2][:middle], "grp_0", 2), shifted(after[2][middle:], "grp_0", -2)]
    )
    near = [block, after[1], after[2], before[2], before[1]]
    return near, [after[3], far, before[3]]


def projected(head_rows, out_block):
    rows, columns = head_rows.shape[0], out_block.shape[1]
    partner = shifted(head_rows, "grp_1", 1)
    products = []
    for gathered in zip(around_the_ring(head_rows), around_the_ring(partner)):
        product = jnp.dot(
            jnp.concatenate(gathered[0] + gathered[1]), out_block, preferred_element_type=jnp.float32
        ).astype(jnp.bfloat16)
        products.append(product.reshape(2, len(gathered[0]), rows, columns))
    near, far = products
    places = jnp.concatenate([near[:, :3], far, near[:, 3:]], axis=1)
    places = rolled(places, lax.axis_index("grp_1"))
    return rolled(jnp.moveaxis(places, 1, 0), lax.axis_index("grp_0"))


def rolled(blocks, count):
    size = blocks.shape[0]
    return lax.dynamic_slice_in_dim(jnp.concatenate([blocks, blocks]), size - count, size, 0)


def own_and_other(array, core, dim):
    size = array.shape[dim] // 2
    return [lax.dynamic_slice_in_dim(array, number * size, size, dim) for number in (core, 1 - core)]


def around_the_ring(block):
    middle = block.shape[0] // 2
    before = {step: shifted(block, "grp_0", step) for step in (2, 1)}
    after = {step: shifted(block, "grp_0", -step) for step in (2, 1)}
    before[3] = shifted(before[2], "grp_0", 1)
    after[3] = shifted(after[2], "grp_0", -1)
    opposite = jnp.concatenate(
        [shifted(before[2][:middle], "grp_0", 2), shifted(after[2][middle:], "grp_0", -2)]
    )
    return [block, after[1], after[2], before[2], before[1]], [after[3], opposite, before[3]]


def projected(head_rows, out_block):
    rows, columns = head_rows.shape[0], out_block.shape[1]
    partner = shifted(head_rows, "grp_1", 1)
    products = []
    for gathered in around_the_ring(jnp.concatenate([head_rows, partner])):
        product = jnp.dot(
            jnp.concatenate(gathered), out_block, preferred_element_type=jnp.float32
        ).astype(jnp.bfloat16)
        product = jnp.pad(product, ((0, 0), (0, -columns % 128)))
        products.append(product.reshape(len(gathered), 2, rows, -1))
    near, far = products
    places = jnp.concatenate([near[:3], far, near[3:]])
    places = rolled(jnp.moveaxis(places, 1, 0), lax.axis_index("grp_1"))
    return rolled(jnp.moveaxis(places, 0, 1), lax.axis_index("grp_0"))


def attention_rows(queries, latent_cache, lengths, w_uv):
    latent_width = w_uv.shape[2]
    query_block = queries[:, :, 0, :]
    scores = (
        jnp.einsum("bhr,bpr->bhp", query_block, latent_cache, preferred_element_type=jnp.float32)
        * score_scale
    )
    positions = jnp.arange(latent_cache.shape[1])
    visible = positions[None, None, :] < lengths[:, None, None]
    scores = jnp.where(visible, scores, -1e30)
    highest = jnp.max(scores, axis=2, keepdims=True)
    raised = jnp.exp(scores - highest)
    softmax_weights = (raised / jnp.sum(raised, axis=2, keepdims=True)).astype(jnp.bfloat16)
    latent_out = jnp.einsum(
        "bhp,bpc->bhc",
        softmax_weights,
        latent_cache[:, :, :latent_width],
        preferred_element_type=jnp.float32,
    ).astype(jnp.bfloat16)
    head_out = jnp.einsum(
        "bhc,hcv->bhv", latent_out, w_uv[:, 0], preferred_element_type=jnp.float32
    ).astype(jnp.bfloat16)
    return head_out.reshape(head_out.shape[0], -1)


def layer(
    hidden_in,
    queries,
    latent_cache,
    lengths,
    w_uv,
    attn_weight,
    norm_gain,
    router,
    routes,
    live_counts,
    expert_in,
    expert_out,
):
    count_of_tokens, width = hidden_in.shape
    groups = lax.axis_size(GRP)
    slices = lax.axis_size(TP)
    chips = lax.axis_size("x")
    chip, core = lax.axis_index("x"), lax.axis_index("core")
    part = width // slices
    slice_width = expert_in.shape[3]

    head_rows = attention_rows(queries, latent_cache, lengths, w_uv)
    head_rows, expert_in = lax.optimization_barrier((head_rows, expert_in))

    rows_of_chip = width // chips
    in_parts = [
        lax.dynamic_slice_in_dim(expert_in[0], (chip + step) % chips * rows_of_chip, rows_of_chip, 0)
        for step in range(chips)
    ]
    in_parts[1:] = [shifted(in_parts[step], "x", step) for step in range(1, chips)]

    out_block = attn_weight[:, 0].reshape(-1, attn_weight.shape[3])
    partial_value = projected(head_rows, out_block)
    partial_value = partial_value.reshape(groups * slices, count_of_tokens, -1)
    partial_value, expert_out = lax.optimization_barrier((partial_value, expert_out))
    arrived = lax.all_to_all(partial_value, GRP_TP, split_axis=0, concat_axis=0, tiled=True)
    out_parts = [
        lax.dynamic_slice_in_dim(expert_out[0], (chip + step) % chips * rows_of_chip, rows_of_chip, 1)
        for step in range(chips)
    ]
    out_parts[1:] = [shifted(out_parts[step], "x", step) for step in range(1, chips)]
    arrived = arrived[:, :, : attn_weight.shape[3]]
    summed = arrived.reshape(groups, slices, count_of_tokens, -1).astype(jnp.float32).sum(axis=1)
    attention = jnp.moveaxis(summed.astype(jnp.bfloat16), 0, 1).reshape(count_of_tokens, width)

    residual = hidden_in.astype(jnp.float32) + attention.astype(jnp.float32)
    normalized_input = (
        residual
        * lax.rsqrt(jnp.mean(residual * residual, axis=1, keepdims=True) + 1e-06)
        * norm_gain
    ).astype(jnp.bfloat16)
    experts = router.shape[1]
    per_token = routes.shape[1]
    capacity = max(2, 2 * count_of_tokens * per_token // experts)
    affinity = jax.nn.sigmoid(jnp.dot(normalized_input, router, preferred_element_type=jnp.float32))
    picked = routes[:, :, None] == jnp.arange(experts)[None, None, :]
    chosen = jnp.sum(jnp.where(picked, affinity[:, None, :], 0.0), axis=2)
    living = jnp.arange(count_of_tokens) < live_counts[0]
    gate_weights = (
        route_scale
        * chosen
        / jnp.sum(chosen, axis=1, keepdims=True)
        * living[:, None].astype(jnp.float32)
    )
    routed = jnp.any(picked, axis=1) & living[:, None]
    routed_count = routed.astype(jnp.int32)
    slot_index = jnp.cumsum(routed_count, axis=0) - routed_count
    placed_tokens = routed[:, :, None] & (
        slot_index[:, :, None] == jnp.arange(capacity)[None, None, :]
    )
    expert_gate = jnp.sum(jnp.where(picked, gate_weights[:, :, None], 0.0), axis=1)
    outgoing = jnp.einsum(
        "poy,ptj->otyj",
        placed_tokens.astype(jnp.bfloat16),
        normalized_input.reshape(count_of_tokens, slices, part),
        preferred_element_type=jnp.float32,
    ).astype(jnp.bfloat16)
    combine_rows = placed_tokens.astype(jnp.float32) * expert_gate[:, :, None]
    outgoing = outgoing.reshape(experts * slices, capacity, part)
    rows = lax.all_to_all(
        outgoing, SEC_GRP_TP, split_axis=0, concat_axis=0, tiled=True
    ).reshape(-1, part)

    in_parts, out_parts, _ = lax.optimization_barrier((in_parts, out_parts, outgoing))
    in_columns = jnp.concatenate(
        [p.reshape(rows_of_chip, 2 * slice_width) for p in in_parts], axis=1
    )
    in_own, in_other = own_and_other(in_columns, core, 0)
    out_own, out_sent = own_and_other(jnp.concatenate(out_parts), core, 1)
    out_other = shifted(out_sent, "core", 1)

    other_rows = shifted(rows, "core", 1)
    products = jnp.dot(rows, in_own, preferred_element_type=jnp.float32) + jnp.dot(
        other_rows, in_other, preferred_element_type=jnp.float32
    )
    products = jnp.split(products, chips, axis=1)
    gate_up = products[0]
    for step in (2, 1, 3):
        block = shifted(products[step].astype(jnp.bfloat16), "x", -step)
        gate_up = gate_up + block.astype(jnp.float32)
    activated = (jax.nn.silu(gate_up[:, :slice_width]) * gate_up[:, slice_width:]).astype(
        jnp.bfloat16
    )
    hidden_own = jnp.concatenate(
        [activated] + [shifted(activated, "x", step) for step in range(1, chips)], axis=1
    )
    hidden_other = shifted(hidden_own, "core", 1)
    values = (
        jnp.dot(hidden_own, out_own, preferred_element_type=jnp.float32)
        + jnp.dot(hidden_other, out_other, preferred_element_type=jnp.float32)
    ).astype(jnp.bfloat16)
    back = lax.all_to_all(
        values.reshape(experts * slices, capacity, part),
        SEC_GRP_TP, split_axis=0, concat_axis=0, tiled=True,
    ).reshape(experts, slices, capacity, part)
    coarse = lax.reduce_precision(combine_rows, 8, 7)
    weights = jnp.concatenate([coarse, combine_rows - coarse], axis=0).astype(jnp.bfloat16)
    mixed = jnp.einsum("poy,otyj->ptj", weights, back, preferred_element_type=jnp.float32)
    expert_mix = (mixed[:count_of_tokens] + mixed[count_of_tokens:]).reshape(count_of_tokens, width)
    return (residual + expert_mix).astype(jnp.bfloat16)


def solution(mesh):
    torus = Mesh(
        mesh.devices.reshape(mesh.shape["sec"], 8, 2, mesh.shape["tp"] // 2, 2), SEC_GRP_TP
    )
    in_specs = (
        P(SEC_GRP_TP, None),
        P(SEC_GRP, None, TP, None),
        P(SEC_GRP, None, None),
        P(SEC_GRP),
        P(None, TP, None, None),
        P(None, TP, None, GRP),
        P(),
        P(),
        P(SEC_GRP_TP, None),
        P(SEC_GRP_TP),
        P(SEC_GRP, None, None, TP),
        P(SEC_GRP, TP, None),
    )
    out_specs = P(SEC_GRP_TP, None)
    return jax.shard_map(layer, mesh=torus, in_specs=in_specs, out_specs=out_specs, check_vma=False)
```

```python
import jax
import jax.numpy as jnp
from jax import lax
from jax.sharding import Mesh
from jax.sharding import PartitionSpec as P


GRP = ("grp_0", "grp_1")
SEC_GRP = ("sec", "grp_0", "grp_1")
TP = ("x", "core")
GRP_TP = ("grp_0", "grp_1", "x", "core")
SEC_GRP_TP = ("sec", "grp_0", "grp_1", "x", "core")


score_scale = 192.0 ** (-0.5)
route_scale = 2.5


def shifted(x, axis, step):
    size = lax.axis_size(axis)
    return lax.ppermute(x, axis, [(i, (i + step) % size) for i in range(size)])


def rolled(blocks, count):
    size = blocks.shape[0]
    return lax.dynamic_slice_in_dim(jnp.concatenate([blocks, blocks]), size - count, size, 0)


def around_the_ring(block):
    middle = block.shape[0] // 2
    before = {step: shifted(block, "grp_0", step) for step in (1, 2)}
    after = {step: shifted(block, "grp_0", -step) for step in (1, 2)}
    before[3] = shifted(before[2], "grp_0", 1)
    after[3] = shifted(after[2], "grp_0", -1)
    far = jnp.concatenate(
        [shifted(before[2][:middle], "grp_0", 2), shifted(after[2][middle:], "grp_0", -2)]
    )
    near = [block, after[1], after[2], before[2], before[1]]
    return near, [after[3], far, before[3]]


def projected(head_rows, out_block):
    rows, columns = head_rows.shape[0], out_block.shape[1]
    partner = shifted(head_rows, "grp_1", 1)
    products = []
    for gathered in zip(around_the_ring(head_rows), around_the_ring(partner)):
        product = jnp.dot(
            jnp.concatenate(gathered[0] + gathered[1]), out_block, preferred_element_type=jnp.float32
        ).astype(jnp.bfloat16)
        products.append(product.reshape(2, len(gathered[0]), rows, columns))
    near, far = products
    places = jnp.concatenate([near[:, :3], far, near[:, 3:]], axis=1)
    places = rolled(places, lax.axis_index("grp_1"))
    return rolled(jnp.moveaxis(places, 1, 0), lax.axis_index("grp_0"))


def rolled(blocks, count):
    size = blocks.shape[0]
    return lax.dynamic_slice_in_dim(jnp.concatenate([blocks, blocks]), size - count, size, 0)


def own_and_other(array, core, dim):
    size = array.shape[dim] // 2
    return [lax.dynamic_slice_in_dim(array, number * size, size, dim) for number in (core, 1 - core)]


def around_the_ring(block):
    middle = block.shape[0] // 2
    before = {step: shifted(block, "grp_0", step) for step in (2, 1)}
    after = {step: shifted(block, "grp_0", -step) for step in (2, 1)}
    before[3] = shifted(before[2], "grp_0", 1)
    after[3] = shifted(after[2], "grp_0", -1)
    opposite = jnp.concatenate(
        [shifted(before[2][:middle], "grp_0", 2), shifted(after[2][middle:], "grp_0", -2)]
    )
    return [block, after[1], after[2], before[2], before[1]], [after[3], opposite, before[3]]


def projected(head_rows, out_block):
    rows, columns = head_rows.shape[0], out_block.shape[1]
    partner = shifted(head_rows, "grp_1", 1)
    products = []
    for gathered in around_the_ring(jnp.concatenate([head_rows, partner])):
        product = jnp.dot(
            jnp.concatenate(gathered), out_block, preferred_element_type=jnp.float32
        ).astype(jnp.bfloat16)
        product = jnp.pad(product, ((0, 0), (0, -columns % 128)))
        products.append(product.reshape(len(gathered), 2, rows, -1))
    near, far = products
    places = jnp.concatenate([near[:3], far, near[3:]])
    places = rolled(jnp.moveaxis(places, 1, 0), lax.axis_index("grp_1"))
    return rolled(jnp.moveaxis(places, 0, 1), lax.axis_index("grp_0"))


def attention_rows(queries, latent_cache, lengths, w_uv):
    latent_width = w_uv.shape[2]
    query_block = queries[:, :, 0, :]
    scores = (
        jnp.einsum("bhr,bpr->bhp", query_block, latent_cache, preferred_element_type=jnp.float32)
        * score_scale
    )
    positions = jnp.arange(latent_cache.shape[1])
    visible = positions[None, None, :] < lengths[:, None, None]
    scores = jnp.where(visible, scores, -1e30)
    highest = jnp.max(scores, axis=2, keepdims=True)
    raised = jnp.exp(scores - highest)
    softmax_weights = (raised / jnp.sum(raised, axis=2, keepdims=True)).astype(jnp.bfloat16)
    latent_out = jnp.einsum(
        "bhp,bpc->bhc",
        softmax_weights,
        latent_cache[:, :, :latent_width],
        preferred_element_type=jnp.float32,
    ).astype(jnp.bfloat16)
    head_out = jnp.einsum(
        "bhc,hcv->bhv", latent_out, w_uv[:, 0], preferred_element_type=jnp.float32
    ).astype(jnp.bfloat16)
    return head_out.reshape(head_out.shape[0], -1)


def layer(
    hidden_in,
    queries,
    latent_cache,
    lengths,
    w_uv,
    attn_weight,
    norm_gain,
    router,
    routes,
    live_counts,
    expert_in,
    expert_out,
):
    count_of_tokens, width = hidden_in.shape
    groups = lax.axis_size(GRP)
    slices = lax.axis_size(TP)
    chips = lax.axis_size("x")
    chip, core = lax.axis_index("x"), lax.axis_index("core")
    part = width // slices
    slice_width = expert_in.shape[3]

    head_rows = attention_rows(queries, latent_cache, lengths, w_uv)
    head_rows, expert_in = lax.optimization_barrier((head_rows, expert_in))

    rows_of_chip = width // chips
    in_parts = [
        lax.dynamic_slice_in_dim(expert_in[0], (chip + step) % chips * rows_of_chip, rows_of_chip, 0)
        for step in range(chips)
    ]
    in_parts[1:] = [shifted(in_parts[step], "x", step) for step in range(1, chips)]

    out_block = attn_weight[:, 0].reshape(-1, attn_weight.shape[3])
    partial_value = projected(head_rows, out_block)
    partial_value = partial_value.reshape(groups * slices, count_of_tokens, -1)
    partial_value, expert_out = lax.optimization_barrier((partial_value, expert_out))
    in_parts, _ = lax.optimization_barrier((in_parts, partial_value))
    in_columns = jnp.concatenate(
        [p.reshape(rows_of_chip, 2 * slice_width) for p in in_parts], axis=1
    )
    arrived = lax.all_to_all(partial_value, GRP_TP, split_axis=0, concat_axis=0, tiled=True)
    out_parts = [
        lax.dynamic_slice_in_dim(expert_out[0], (chip + step) % chips * rows_of_chip, rows_of_chip, 1)
        for step in range(chips)
    ]
    out_parts[1:] = [shifted(out_parts[step], "x", step) for step in range(1, chips)]
    arrived = arrived[:, :, : attn_weight.shape[3]]
    summed = arrived.reshape(groups, slices, count_of_tokens, -1).astype(jnp.float32).sum(axis=1)
    attention = jnp.moveaxis(summed.astype(jnp.bfloat16), 0, 1).reshape(count_of_tokens, width)

    residual = hidden_in.astype(jnp.float32) + attention.astype(jnp.float32)
    normalized_input = (
        residual
        * lax.rsqrt(jnp.mean(residual * residual, axis=1, keepdims=True) + 1e-06)
        * norm_gain
    ).astype(jnp.bfloat16)
    experts = router.shape[1]
    per_token = routes.shape[1]
    capacity = max(2, 2 * count_of_tokens * per_token // experts)
    picked = routes[:, :, None] == jnp.arange(experts)[None, None, :]
    living = jnp.arange(count_of_tokens) < live_counts[0]
    routed = jnp.any(picked, axis=1) & living[:, None]
    routed_count = routed.astype(jnp.int32)
    slot_index = jnp.cumsum(routed_count, axis=0) - routed_count
    placed_tokens = routed[:, :, None] & (
        slot_index[:, :, None] == jnp.arange(capacity)[None, None, :]
    )
    outgoing = jnp.einsum(
        "poy,ptj->otyj",
        placed_tokens.astype(jnp.bfloat16),
        normalized_input.reshape(count_of_tokens, slices, part),
        preferred_element_type=jnp.float32,
    ).astype(jnp.bfloat16)
    outgoing = outgoing.reshape(experts * slices, capacity, part)
    outgoing, in_columns = lax.optimization_barrier((outgoing, in_columns))
    in_own, in_other = own_and_other(in_columns, core, 0)
    arrived_rows = lax.all_to_all(
        outgoing, SEC_GRP_TP, split_axis=0, concat_axis=0, tiled=True
    )

    out_parts, _ = lax.optimization_barrier((out_parts, outgoing))
    out_own, out_sent = own_and_other(jnp.concatenate(out_parts), core, 1)
    out_other = shifted(out_sent, "core", 1)
    arrived_rows, out_own, out_other = lax.optimization_barrier((arrived_rows, out_own, out_other))

    placed_late, _ = lax.optimization_barrier((placed_tokens, outgoing))
    logits = jnp.dot(normalized_input, router, preferred_element_type=jnp.float32)
    affinity = jax.nn.sigmoid(logits)
    chosen = jnp.sum(jnp.where(picked, affinity[:, None, :], 0.0), axis=2)
    gate_weights = (
        route_scale
        * chosen
        / jnp.sum(chosen, axis=1, keepdims=True)
        * living[:, None].astype(jnp.float32)
    )
    expert_gate = jnp.sum(jnp.where(picked, gate_weights[:, :, None], 0.0), axis=1)
    combine_rows = placed_late.astype(jnp.float32) * expert_gate[:, :, None]

    other_rows = shifted(arrived_rows, "core", 1).reshape(-1, part)
    rows = arrived_rows.reshape(-1, part)
    products = jnp.dot(rows, in_own, preferred_element_type=jnp.float32) + jnp.dot(
        other_rows, in_other, preferred_element_type=jnp.float32
    )
    products = jnp.split(products, chips, axis=1)
    gate_up = products[0]
    for step in (2, 1, 3):
        block = shifted(products[step].astype(jnp.bfloat16), "x", -step)
        gate_up = gate_up + block.astype(jnp.float32)
    activated = (jax.nn.silu(gate_up[:, :slice_width]) * gate_up[:, slice_width:]).astype(
        jnp.bfloat16
    )
    hidden_own = jnp.concatenate(
        [activated] + [shifted(activated, "x", step) for step in range(1, chips)], axis=1
    )
    hidden_other = shifted(hidden_own, "core", 1)
    values = (
        jnp.dot(hidden_own, out_own, preferred_element_type=jnp.float32)
        + jnp.dot(hidden_other, out_other, preferred_element_type=jnp.float32)
    ).astype(jnp.bfloat16)
    back = lax.all_to_all(
        values.reshape(experts * slices, capacity, part),
        SEC_GRP_TP, split_axis=0, concat_axis=0, tiled=True,
    ).reshape(experts, slices, capacity, part)
    coarse = lax.reduce_precision(combine_rows, 8, 7)
    weights = jnp.concatenate([coarse, combine_rows - coarse], axis=0).astype(jnp.bfloat16)
    mixed = jnp.einsum("poy,otyj->ptj", weights, back, preferred_element_type=jnp.float32)
    expert_mix = (mixed[:count_of_tokens] + mixed[count_of_tokens:]).reshape(count_of_tokens, width)
    return (residual + expert_mix).astype(jnp.bfloat16)


def solution(mesh):
    torus = Mesh(
        mesh.devices.reshape(mesh.shape["sec"], 8, 2, mesh.shape["tp"] // 2, 2), SEC_GRP_TP
    )
    in_specs = (
        P(SEC_GRP_TP, None),
        P(SEC_GRP, None, TP, None),
        P(SEC_GRP, None, None),
        P(SEC_GRP),
        P(None, TP, None, None),
        P(None, TP, None, GRP),
        P(),
        P(),
        P(SEC_GRP_TP, None),
        P(SEC_GRP_TP),
        P(SEC_GRP, None, None, TP),
        P(SEC_GRP, TP, None),
    )
    out_specs = P(SEC_GRP_TP, None)
    return jax.shard_map(layer, mesh=torus, in_specs=in_specs, out_specs=out_specs, check_vma=False)
```

```python
import jax
import jax.numpy as jnp
from jax import lax
from jax.sharding import Mesh
from jax.sharding import PartitionSpec as P


GRP = ("grp_0", "grp_1")
SEC_GRP = ("sec", "grp_0", "grp_1")
TP = ("x", "core")
GRP_TP = ("grp_0", "grp_1", "x", "core")
SEC_GRP_TP = ("sec", "grp_0", "grp_1", "x", "core")


score_scale = 192.0 ** (-0.5)
route_scale = 2.5


def shifted(x, axis, step):
    size = lax.axis_size(axis)
    return lax.ppermute(x, axis, [(i, (i + step) % size) for i in range(size)])


def rolled(blocks, count):
    size = blocks.shape[0]
    return lax.dynamic_slice_in_dim(jnp.concatenate([blocks, blocks]), size - count, size, 0)


def around_the_ring(block):
    middle = block.shape[0] // 2
    before = {step: shifted(block, "grp_0", step) for step in (1, 2)}
    after = {step: shifted(block, "grp_0", -step) for step in (1, 2)}
    before[3] = shifted(before[2], "grp_0", 1)
    after[3] = shifted(after[2], "grp_0", -1)
    far = jnp.concatenate(
        [shifted(before[2][:middle], "grp_0", 2), shifted(after[2][middle:], "grp_0", -2)]
    )
    near = [block, after[1], after[2], before[2], before[1]]
    return near, [after[3], far, before[3]]


def projected(head_rows, out_block):
    rows, columns = head_rows.shape[0], out_block.shape[1]
    partner = shifted(head_rows, "grp_1", 1)
    products = []
    for gathered in zip(around_the_ring(head_rows), around_the_ring(partner)):
        product = jnp.dot(
            jnp.concatenate(gathered[0] + gathered[1]), out_block, preferred_element_type=jnp.float32
        ).astype(jnp.bfloat16)
        products.append(product.reshape(2, len(gathered[0]), rows, columns))
    near, far = products
    places = jnp.concatenate([near[:, :3], far, near[:, 3:]], axis=1)
    places = rolled(places, lax.axis_index("grp_1"))
    return rolled(jnp.moveaxis(places, 1, 0), lax.axis_index("grp_0"))


def rolled(blocks, count):
    size = blocks.shape[0]
    return lax.dynamic_slice_in_dim(jnp.concatenate([blocks, blocks]), size - count, size, 0)


def own_and_other(array, core, dim):
    size = array.shape[dim] // 2
    return [lax.dynamic_slice_in_dim(array, number * size, size, dim) for number in (core, 1 - core)]


def around_the_ring(block):
    middle = block.shape[0] // 2
    before = {step: shifted(block, "grp_0", step) for step in (2, 1)}
    after = {step: shifted(block, "grp_0", -step) for step in (2, 1)}
    before[3] = shifted(before[2], "grp_0", 1)
    after[3] = shifted(after[2], "grp_0", -1)
    opposite = jnp.concatenate(
        [shifted(before[2][:middle], "grp_0", 2), shifted(after[2][middle:], "grp_0", -2)]
    )
    return [block, after[1], after[2], before[2], before[1]], [after[3], opposite, before[3]]


def projected(head_rows, out_block):
    rows, columns = head_rows.shape[0], out_block.shape[1]
    partner = shifted(head_rows, "grp_1", 1)
    products = []
    for gathered in around_the_ring(jnp.concatenate([head_rows, partner])):
        product = jnp.dot(
            jnp.concatenate(gathered), out_block, preferred_element_type=jnp.float32
        ).astype(jnp.bfloat16)
        product = jnp.pad(product, ((0, 0), (0, -columns % 128)))
        products.append(product.reshape(len(gathered), 2, rows, -1))
    near, far = products
    places = jnp.concatenate([near[:3], far, near[3:]])
    places = rolled(jnp.moveaxis(places, 1, 0), lax.axis_index("grp_1"))
    return rolled(jnp.moveaxis(places, 0, 1), lax.axis_index("grp_0"))


def attention_rows(queries, latent_cache, lengths, w_uv):
    latent_width = w_uv.shape[2]
    query_block = queries[:, :, 0, :]
    scores = (
        jnp.einsum("bhr,bpr->bhp", query_block, latent_cache, preferred_element_type=jnp.float32)
        * score_scale
    )
    positions = jnp.arange(latent_cache.shape[1])
    visible = positions[None, None, :] < lengths[:, None, None]
    scores = jnp.where(visible, scores, -1e30)
    highest = jnp.max(scores, axis=2, keepdims=True)
    raised = jnp.exp(scores - highest)
    softmax_weights = (raised / jnp.sum(raised, axis=2, keepdims=True)).astype(jnp.bfloat16)
    latent_out = jnp.einsum(
        "bhp,bpc->bhc",
        softmax_weights,
        latent_cache[:, :, :latent_width],
        preferred_element_type=jnp.float32,
    ).astype(jnp.bfloat16)
    head_out = jnp.einsum(
        "bhc,hcv->bhv", latent_out, w_uv[:, 0], preferred_element_type=jnp.float32
    ).astype(jnp.bfloat16)
    return head_out.reshape(head_out.shape[0], -1)


def layer(
    hidden_in,
    queries,
    latent_cache,
    lengths,
    w_uv,
    attn_weight,
    norm_gain,
    router,
    routes,
    live_counts,
    expert_in,
    expert_out,
):
    count_of_tokens, width = hidden_in.shape
    groups = lax.axis_size(GRP)
    slices = lax.axis_size(TP)
    chips = lax.axis_size("x")
    chip, core = lax.axis_index("x"), lax.axis_index("core")
    part = width // slices
    slice_width = expert_in.shape[3]

    head_rows = attention_rows(queries, latent_cache, lengths, w_uv)
    head_rows, expert_in = lax.optimization_barrier((head_rows, expert_in))

    rows_of_chip = width // chips
    in_parts = [
        lax.dynamic_slice_in_dim(expert_in[0], (chip + step) % chips * rows_of_chip, rows_of_chip, 0)
        for step in range(chips)
    ]
    in_parts[1:] = [shifted(in_parts[step], "x", step) for step in range(1, chips)]

    out_block = attn_weight[:, 0].reshape(-1, attn_weight.shape[3])
    partial_value = projected(head_rows, out_block)
    partial_value = partial_value.reshape(groups * slices, count_of_tokens, -1)
    partial_value, expert_out = lax.optimization_barrier((partial_value, expert_out))
    in_parts, _ = lax.optimization_barrier((in_parts, partial_value))
    in_columns = jnp.concatenate(
        [p.reshape(rows_of_chip, 2 * slice_width) for p in in_parts], axis=1
    )
    arrived = lax.all_to_all(partial_value, GRP_TP, split_axis=0, concat_axis=0, tiled=True)
    out_parts = [
        lax.dynamic_slice_in_dim(expert_out[0], (chip + step) % chips * rows_of_chip, rows_of_chip, 1)
        for step in range(chips)
    ]
    out_parts[1:] = [shifted(out_parts[step], "x", step) for step in range(1, chips)]
    arrived = arrived[:, :, : attn_weight.shape[3]]
    summed = arrived.reshape(groups, slices, count_of_tokens, -1).astype(jnp.float32).sum(axis=1)
    attention = jnp.moveaxis(summed.astype(jnp.bfloat16), 0, 1).reshape(count_of_tokens, width)

    residual = hidden_in.astype(jnp.float32) + attention.astype(jnp.float32)
    normalized_input = (
        residual
        * lax.rsqrt(jnp.mean(residual * residual, axis=1, keepdims=True) + 1e-06)
        * norm_gain
    ).astype(jnp.bfloat16)
    experts = router.shape[1]
    per_token = routes.shape[1]
    capacity = max(2, 2 * count_of_tokens * per_token // experts)
    picked = routes[:, :, None] == jnp.arange(experts)[None, None, :]
    living = jnp.arange(count_of_tokens) < live_counts[0]
    routed = jnp.any(picked, axis=1) & living[:, None]
    routed_count = routed.astype(jnp.int32)
    slot_index = jnp.cumsum(routed_count, axis=0) - routed_count
    placed_tokens = routed[:, :, None] & (
        slot_index[:, :, None] == jnp.arange(capacity)[None, None, :]
    )
    outgoing = jnp.einsum(
        "poy,ptj->otyj",
        placed_tokens.astype(jnp.bfloat16),
        normalized_input.reshape(count_of_tokens, slices, part),
        preferred_element_type=jnp.float32,
    ).astype(jnp.bfloat16)
    outgoing = outgoing.reshape(experts * slices, capacity, part)
    outgoing, in_columns = lax.optimization_barrier((outgoing, in_columns))
    in_own, in_other = own_and_other(in_columns, core, 0)
    arrived_rows = lax.all_to_all(
        outgoing, SEC_GRP_TP, split_axis=0, concat_axis=0, tiled=True
    )

    rows = arrived_rows.reshape(-1, part)
    other_rows = shifted(rows, "core", 1)
    products = jnp.dot(rows, in_own, preferred_element_type=jnp.float32) + jnp.dot(
        other_rows, in_other, preferred_element_type=jnp.float32
    )
    products = jnp.split(products, chips, axis=1)
    sent = {step: products[step].astype(jnp.bfloat16) for step in (2, 1, 3)}
    gate_up = products[0]
    for step, block in sent.items():
        gate_up = gate_up + shifted(block, "x", -step).astype(jnp.float32)
    out_parts, _ = lax.optimization_barrier((out_parts, sent[1]))
    out_own, out_sent = own_and_other(jnp.concatenate(out_parts), core, 1)
    out_other = shifted(out_sent, "core", 1)
    activated = (jax.nn.silu(gate_up[:, :slice_width]) * gate_up[:, slice_width:]).astype(
        jnp.bfloat16
    )
    hidden_own = jnp.concatenate(
        [activated] + [shifted(activated, "x", step) for step in range(1, chips)], axis=1
    )
    hidden_other = shifted(hidden_own, "core", 1)
    values = (
        jnp.dot(hidden_own, out_own, preferred_element_type=jnp.float32)
        + jnp.dot(hidden_other, out_other, preferred_element_type=jnp.float32)
    ).astype(jnp.bfloat16)
    values = values.reshape(experts * slices, capacity, part)
    back = lax.all_to_all(values, SEC_GRP_TP, split_axis=0, concat_axis=0, tiled=True)
    back = back.reshape(experts, slices, capacity, part)

    placed_late, _ = lax.optimization_barrier((placed_tokens, values))
    logits = jnp.dot(normalized_input, router, preferred_element_type=jnp.float32)
    affinity = jax.nn.sigmoid(logits)
    chosen = jnp.sum(jnp.where(picked, affinity[:, None, :], 0.0), axis=2)
    gate_weights = (
        route_scale
        * chosen
        / jnp.sum(chosen, axis=1, keepdims=True)
        * living[:, None].astype(jnp.float32)
    )
    expert_gate = jnp.sum(jnp.where(picked, gate_weights[:, :, None], 0.0), axis=1)
    combine_rows = placed_late.astype(jnp.float32) * expert_gate[:, :, None]

    coarse = lax.reduce_precision(combine_rows, 8, 7)
    weights = jnp.concatenate([coarse, combine_rows - coarse], axis=0).astype(jnp.bfloat16)
    mixed = jnp.einsum("poy,otyj->ptj", weights, back, preferred_element_type=jnp.float32)
    expert_mix = (mixed[:count_of_tokens] + mixed[count_of_tokens:]).reshape(count_of_tokens, width)
    return (residual + expert_mix).astype(jnp.bfloat16)


def solution(mesh):
    torus = Mesh(
        mesh.devices.reshape(mesh.shape["sec"], 8, 2, mesh.shape["tp"] // 2, 2), SEC_GRP_TP
    )
    in_specs = (
        P(SEC_GRP_TP, None),
        P(SEC_GRP, None, TP, None),
        P(SEC_GRP, None, None),
        P(SEC_GRP),
        P(None, TP, None, None),
        P(None, TP, None, GRP),
        P(),
        P(),
        P(SEC_GRP_TP, None),
        P(SEC_GRP_TP),
        P(SEC_GRP, None, None, TP),
        P(SEC_GRP, TP, None),
    )
    out_specs = P(SEC_GRP_TP, None)
    return jax.shard_map(layer, mesh=torus, in_specs=in_specs, out_specs=out_specs, check_vma=False)
```

```python
import jax
import jax.numpy as jnp
from jax import lax
from jax.sharding import Mesh
from jax.sharding import PartitionSpec as P


GRP = ("grp_0", "grp_1")
SEC_GRP = ("sec", "grp_0", "grp_1")
TP = ("x", "core")
GRP_TP = ("grp_0", "grp_1", "x", "core")
TP_SEC_GRP = ("x", "core", "sec", "grp_0", "grp_1")
SEC_GRP_TP = ("sec", "grp_0", "grp_1", "x", "core")


score_scale = 192.0 ** (-0.5)
route_scale = 2.5


def shifted(x, axis, step):
    size = lax.axis_size(axis)
    return lax.ppermute(x, axis, [(i, (i + step) % size) for i in range(size)])


def rolled(blocks, count):
    size = blocks.shape[0]
    return lax.dynamic_slice_in_dim(jnp.concatenate([blocks, blocks]), size - count, size, 0)


def around_the_ring(block):
    middle = block.shape[0] // 2
    before = {step: shifted(block, "grp_0", step) for step in (1, 2)}
    after = {step: shifted(block, "grp_0", -step) for step in (1, 2)}
    before[3] = shifted(before[2], "grp_0", 1)
    after[3] = shifted(after[2], "grp_0", -1)
    far = jnp.concatenate(
        [shifted(before[2][:middle], "grp_0", 2), shifted(after[2][middle:], "grp_0", -2)]
    )
    near = [block, after[1], after[2], before[2], before[1]]
    return near, [after[3], far, before[3]]


def projected(head_rows, out_block):
    rows, columns = head_rows.shape[0], out_block.shape[1]
    partner = shifted(head_rows, "grp_1", 1)
    products = []
    for gathered in zip(around_the_ring(head_rows), around_the_ring(partner)):
        product = jnp.dot(
            jnp.concatenate(gathered[0] + gathered[1]), out_block, preferred_element_type=jnp.float32
        ).astype(jnp.bfloat16)
        products.append(product.reshape(2, len(gathered[0]), rows, columns))
    near, far = products
    places = jnp.concatenate([near[:, :3], far, near[:, 3:]], axis=1)
    places = rolled(places, lax.axis_index("grp_1"))
    return rolled(jnp.moveaxis(places, 1, 0), lax.axis_index("grp_0"))


def rolled(blocks, count):
    size = blocks.shape[0]
    return lax.dynamic_slice_in_dim(jnp.concatenate([blocks, blocks]), size - count, size, 0)


def own_and_other(array, core, dim):
    size = array.shape[dim] // 2
    return [lax.dynamic_slice_in_dim(array, number * size, size, dim) for number in (core, 1 - core)]


def around_the_ring(block):
    middle = block.shape[0] // 2
    before = {step: shifted(block, "grp_0", step) for step in (2, 1)}
    after = {step: shifted(block, "grp_0", -step) for step in (2, 1)}
    before[3] = shifted(before[2], "grp_0", 1)
    after[3] = shifted(after[2], "grp_0", -1)
    opposite = jnp.concatenate(
        [shifted(before[2][:middle], "grp_0", 2), shifted(after[2][middle:], "grp_0", -2)]
    )
    return [block, after[1], after[2], before[2], before[1]], [after[3], opposite, before[3]]


def projected(head_rows, out_block):
    rows, columns = head_rows.shape[0], out_block.shape[1]
    partner = shifted(head_rows, "grp_1", 1)
    products = []
    for gathered in around_the_ring(jnp.concatenate([head_rows, partner])):
        product = jnp.dot(
            jnp.concatenate(gathered), out_block, preferred_element_type=jnp.float32
        ).astype(jnp.bfloat16)
        product = jnp.pad(product, ((0, 0), (0, -columns % 128)))
        products.append(product.reshape(len(gathered), 2, rows, -1))
    near, far = products
    places = jnp.concatenate([near[:3], far, near[3:]])
    places = rolled(jnp.moveaxis(places, 1, 0), lax.axis_index("grp_1"))
    return rolled(jnp.moveaxis(places, 0, 1), lax.axis_index("grp_0"))


def attention_rows(queries, latent_cache, lengths, w_uv):
    latent_width = w_uv.shape[2]
    query_block = queries[:, :, 0, :]
    scores = (
        jnp.einsum("bhr,bpr->bhp", query_block, latent_cache, preferred_element_type=jnp.float32)
        * score_scale
    )
    positions = jnp.arange(latent_cache.shape[1])
    visible = positions[None, None, :] < lengths[:, None, None]
    scores = jnp.where(visible, scores, -1e30)
    highest = jnp.max(scores, axis=2, keepdims=True)
    raised = jnp.exp(scores - highest)
    softmax_weights = (raised / jnp.sum(raised, axis=2, keepdims=True)).astype(jnp.bfloat16)
    latent_out = jnp.einsum(
        "bhp,bpc->bhc",
        softmax_weights,
        latent_cache[:, :, :latent_width],
        preferred_element_type=jnp.float32,
    ).astype(jnp.bfloat16)
    head_out = jnp.einsum(
        "bhc,hcv->bhv", latent_out, w_uv[:, 0], preferred_element_type=jnp.float32
    ).astype(jnp.bfloat16)
    return head_out.reshape(head_out.shape[0], -1)


def layer(
    hidden_in,
    queries,
    latent_cache,
    lengths,
    w_uv,
    attn_weight,
    norm_gain,
    router,
    routes,
    live_counts,
    expert_in,
    expert_out,
):
    count_of_tokens, width = hidden_in.shape
    groups = lax.axis_size(GRP)
    slices = lax.axis_size(TP)
    chips = lax.axis_size("x")
    chip, core = lax.axis_index("x"), lax.axis_index("core")
    part = width // slices
    slice_width = expert_in.shape[3]

    head_rows = attention_rows(queries, latent_cache, lengths, w_uv)
    head_rows, expert_in = lax.optimization_barrier((head_rows, expert_in))

    rows_of_chip = width // chips
    in_parts = [
        lax.dynamic_slice_in_dim(expert_in[0], (chip + step) % chips * rows_of_chip, rows_of_chip, 0)
        for step in range(chips)
    ]
    in_parts[1:] = [shifted(in_parts[step], "x", step) for step in range(1, chips)]

    out_block = attn_weight[:, 0].reshape(-1, attn_weight.shape[3])
    partial_value = projected(head_rows, out_block)
    partial_value = partial_value.reshape(groups * slices, count_of_tokens, -1)
    partial_value, expert_out = lax.optimization_barrier((partial_value, expert_out))
    in_parts, _ = lax.optimization_barrier((in_parts, partial_value))
    in_columns = jnp.concatenate(
        [p.reshape(rows_of_chip, 2 * slice_width) for p in in_parts], axis=1
    )
    arrived = lax.all_to_all(partial_value, GRP_TP, split_axis=0, concat_axis=0, tiled=True)
    out_parts = [
        lax.dynamic_slice_in_dim(expert_out[0], (chip + step) % chips * rows_of_chip, rows_of_chip, 1)
        for step in range(chips)
    ]
    out_parts[1:] = [shifted(out_parts[step], "x", step) for step in range(1, chips)]
    arrived = arrived[:, :, : attn_weight.shape[3]]
    summed = arrived.reshape(groups, slices, count_of_tokens, -1).astype(jnp.float32).sum(axis=1)
    attention = jnp.moveaxis(summed.astype(jnp.bfloat16), 0, 1).reshape(count_of_tokens, width)

    residual = hidden_in.astype(jnp.float32) + attention.astype(jnp.float32)
    normalized_input = (
        residual
        * lax.rsqrt(jnp.mean(residual * residual, axis=1, keepdims=True) + 1e-06)
        * norm_gain
    ).astype(jnp.bfloat16)
    experts = router.shape[1]
    per_token = routes.shape[1]
    capacity = max(2, 2 * count_of_tokens * per_token // experts)
    picked = routes[:, :, None] == jnp.arange(experts)[None, None, :]
    living = jnp.arange(count_of_tokens) < live_counts[0]
    routed = jnp.any(picked, axis=1) & living[:, None]
    routed_count = routed.astype(jnp.int32)
    slot_index = jnp.cumsum(routed_count, axis=0) - routed_count
    placed_tokens = routed[:, :, None] & (
        slot_index[:, :, None] == jnp.arange(capacity)[None, None, :]
    )
    outgoing = jnp.einsum(
        "poy,ptj->toyj",
        placed_tokens.astype(jnp.bfloat16),
        normalized_input.reshape(count_of_tokens, slices, part),
        preferred_element_type=jnp.float32,
    ).astype(jnp.bfloat16)
    outgoing = outgoing.reshape(slices * experts, capacity, part)
    outgoing, in_columns = lax.optimization_barrier((outgoing, in_columns))
    in_own, in_other = own_and_other(in_columns, core, 0)
    arrived_rows = lax.all_to_all(
        outgoing, TP_SEC_GRP, split_axis=0, concat_axis=0, tiled=True
    )

    rows = arrived_rows.reshape(-1, part)
    other_rows = shifted(rows, "core", 1)
    products = jnp.dot(rows, in_own, preferred_element_type=jnp.float32) + jnp.dot(
        other_rows, in_other, preferred_element_type=jnp.float32
    )
    products = jnp.split(products, chips, axis=1)
    sent = {step: products[step].astype(jnp.bfloat16) for step in (2, 1, 3)}
    gate_up = products[0]
    for step, block in sent.items():
        gate_up = gate_up + shifted(block, "x", -step).astype(jnp.float32)
    out_parts, _ = lax.optimization_barrier((out_parts, sent[1]))
    out_own, out_sent = own_and_other(jnp.concatenate(out_parts), core, 1)
    out_other = shifted(out_sent, "core", 1)
    activated = (jax.nn.silu(gate_up[:, :slice_width]) * gate_up[:, slice_width:]).astype(
        jnp.bfloat16
    )
    hidden_own = jnp.concatenate(
        [activated] + [shifted(activated, "x", step) for step in range(1, chips)], axis=1
    )
    hidden_other = shifted(hidden_own, "core", 1)
    values = (
        jnp.dot(hidden_own, out_own, preferred_element_type=jnp.float32)
        + jnp.dot(hidden_other, out_other, preferred_element_type=jnp.float32)
    ).astype(jnp.bfloat16)
    values = values.reshape(slices * experts, capacity, part)
    back = lax.all_to_all(values, TP_SEC_GRP, split_axis=0, concat_axis=0, tiled=True)
    back = back.reshape(slices, experts, capacity, part)

    placed_late, _ = lax.optimization_barrier((placed_tokens, values))
    logits = jnp.dot(normalized_input, router, preferred_element_type=jnp.float32)
    affinity = jax.nn.sigmoid(logits)
    chosen = jnp.sum(jnp.where(picked, affinity[:, None, :], 0.0), axis=2)
    gate_weights = (
        route_scale
        * chosen
        / jnp.sum(chosen, axis=1, keepdims=True)
        * living[:, None].astype(jnp.float32)
    )
    expert_gate = jnp.sum(jnp.where(picked, gate_weights[:, :, None], 0.0), axis=1)
    combine_rows = placed_late.astype(jnp.float32) * expert_gate[:, :, None]

    coarse = lax.reduce_precision(combine_rows, 8, 7)
    weights = jnp.concatenate([coarse, combine_rows - coarse], axis=0).astype(jnp.bfloat16)
    mixed = jnp.einsum("poy,toyj->ptj", weights, back, preferred_element_type=jnp.float32)
    expert_mix = (mixed[:count_of_tokens] + mixed[count_of_tokens:]).reshape(count_of_tokens, width)
    return (residual + expert_mix).astype(jnp.bfloat16)


def solution(mesh):
    torus = Mesh(
        mesh.devices.reshape(mesh.shape["sec"], 8, 2, mesh.shape["tp"] // 2, 2), SEC_GRP_TP
    )
    in_specs = (
        P(SEC_GRP_TP, None),
        P(SEC_GRP, None, TP, None),
        P(SEC_GRP, None, None),
        P(SEC_GRP),
        P(None, TP, None, None),
        P(None, TP, None, GRP),
        P(),
        P(),
        P(SEC_GRP_TP, None),
        P(SEC_GRP_TP),
        P(SEC_GRP, None, None, TP),
        P(SEC_GRP, TP, None),
    )
    out_specs = P(SEC_GRP_TP, None)
    return jax.shard_map(layer, mesh=torus, in_specs=in_specs, out_specs=out_specs, check_vma=False)
```
